128 devices in a mesh: guide: 2 (over core), kv: 4 (over y), seq: 16 (over z, x).
Axes of the slice: x: 4, y: 4, z: 4, core: 2. Of those that a mesh axis runs over, the one named last changes fastest.
Arguments:
- hidden: bfloat16 [2, 8, 4608], P(None, None, ('guide', 'seq')), may hold values from -50 to 50
- lengths: int32 [2, 8], replicated, may hold values from 1 to 8192, as said below
- slot_owner: int32 [2, 8], replicated, may hold values from 0 to 7, each once within a row
- allowed_ids: int32 [65536], P(('kv', 'seq')), may hold values from 0 to 131071, as said below
- guidance: float32 [8], replicated, may hold values from 1 to 4
- pre_attn_gain: float32 [4608], P(('guide', 'seq')), may hold values from 0.1 to 1.9
- post_attn_gain: float32 [4608], P(('guide', 'seq')), may hold values from 0.4 to 2.1
- pre_ffw_gain: float32 [4608], P(('guide', 'seq')), may hold values from 0.1 to 1.9
- post_ffw_gain: float32 [4608], P(('guide', 'seq')), may hold values from 0.4 to 2.1
- final_gain: float32 [4608], P(('guide', 'seq')), may hold values from 0.1 to 1.9
- query_weight: bfloat16 [4608, 4096], P(('guide', 'seq'), 'kv'), may hold values from -0.09375 to 0.09375
- key_weight: bfloat16 [4608, 2048], P(('guide', 'seq'), 'kv'), may hold values from -0.09375 to 0.09375
- value_weight: bfloat16 [4608, 2048], P(('guide', 'seq'), 'kv'), may hold values from -0.09375 to 0.09375
- output_weight: bfloat16 [4096, 4608], P('kv', ('guide', 'seq')), may hold values from -1 to 1
- gate_weight: bfloat16 [4608, 36864], P(('guide', 'seq'), 'kv'), may hold values from -1 to 1
- up_weight: bfloat16 [4608, 36864], P(('guide', 'seq'), 'kv'), may hold values from -1 to 1
- down_weight: bfloat16 [36864, 4608], P('kv', ('guide', 'seq')), may hold values from -1 to 1
- embedding: bfloat16 [131072, 4608], P(('kv', 'seq'), 'guide'), may hold values from -1 to 1
- cond_keys: bfloat16 [8, 8192, 2048], P(None, ('guide', 'seq'), 'kv'), may hold values from -6 to 6
- cond_values: bfloat16 [8, 8192, 2048], P(None, ('guide', 'seq'), 'kv'), may hold values from -6 to 6
- uncond_keys: bfloat16 [8, 2048, 2048], P(None, ('guide', 'seq'), 'kv'), may hold values from -6 to 6
- uncond_values: bfloat16 [8, 2048, 2048], P(None, ('guide', 'seq'), 'kv'), may hold values from -6 to 6
Outputs:
- mixed: float32 [8, 65536], P('guide', ('kv', 'seq'))
The draws below stay inside these ranges and needn't reach their ends.
Inputs may be any that keep to these rules, and one draw needn't show every extreme that they name: lengths[0] lies in 1 to 8192 and some request has exactly 8192; lengths[1] lies in 1 to 2048 and some request has exactly 2048. `slot_owner`: each row is a permutation of the 8 requests. `allowed_ids`: the ids of the i-th aligned block of 1024 entries are distinct and lie in rows i * 2048 to (i + 1) * 2048 - 1 of the table.
All inputs are finite; a program needn't handle non-finite values.
Results may differ from the reference program's by a relative error of at most 0.0039.
Values may be sent and summed in bfloat16 or wider, within the bound.
A program may use at most 128 MiB of HBM per device.

```python
import jax
import jax.numpy as jnp
from jax import lax

D = 4608
H = 32
KVH = 16
HD = 128
FF = 36864
VOCAB = 131072
ALLOWED = 65536
CAP = 8192
UCAP = 2048
R = 8
VBLOCKS = 64
VROWS = 2048
ABLOCK = 1024


PROFILE_RMS = 1.4662


def profile(key):
    base_key = jax.random.fold_in(key, 7001)
    size_key = jax.random.fold_in(base_key, 1)
    sign_key = jax.random.fold_in(base_key, 2)
    magnitude = 10.0 ** jax.random.uniform(size_key, (D,), dtype=jnp.float32, minval=-0.5, maxval=0.5)
    signs = jnp.where(jax.random.bernoulli(sign_key, 0.5, (D,)), 1.0, -1.0).astype(jnp.float32)
    return (magnitude, signs * magnitude / PROFILE_RMS)


def clipped_normal(key, shape, limit):
    return jnp.clip(jax.random.normal(key, shape, dtype=jnp.float32), -limit, limit)


def draw_hidden(key, part):
    magnitude, direction = profile(key)
    rough_key = jax.random.fold_in(key, 11)
    row_key = jax.random.fold_in(key, 12)
    column_scale = 10.0 ** (jnp.arange(D, dtype=jnp.float32) / D)
    row_scale = 10.0 ** jax.random.uniform(row_key, (2, R, 1), dtype=jnp.float32)
    base = jnp.clip(jax.random.normal(rough_key, (2, R, D), dtype=jnp.float32), -4.0, 4.0)
    return (row_scale * (0.1 * base * column_scale + 0.4 * direction)).astype(jnp.bfloat16)


def draw_lengths(key, part):
    cond_key = jax.random.fold_in(key, 21)
    uncond_key = jax.random.fold_in(key, 22)
    pick_key = jax.random.fold_in(key, 23)
    cond_len = jax.random.randint(cond_key, (R,), 1, CAP + 1)
    uncond_len = jax.random.randint(uncond_key, (R,), 1, UCAP + 1)
    picked = jax.random.randint(pick_key, (2,), 0, R)
    places = jnp.arange(R, dtype=jnp.int32)
    cond_len = jnp.where(places == picked[0], CAP, cond_len)
    uncond_len = jnp.where(places == picked[1], UCAP, uncond_len)
    return jnp.stack([cond_len, uncond_len]).astype(jnp.int32)


def draw_allowed_ids(key, part):
    noise = jax.random.randint(jax.random.fold_in(key, 31), (VBLOCKS, VROWS), 0, (1 << 30) // VROWS)
    local_rows = jnp.arange(VROWS, dtype=jnp.int32)
    scores = noise * VROWS + local_rows[None, :]
    scores = jnp.where(local_rows[None, :] == 0, -2, scores)
    scores = jnp.where(local_rows[None, :] == VROWS - 1, -1, scores)
    order = jnp.argsort(scores, axis=1)[:, :ABLOCK].astype(jnp.int32)
    block_first = (jnp.arange(VBLOCKS, dtype=jnp.int32) * VROWS)[:, None]
    return (order + block_first).reshape(ALLOWED).astype(jnp.int32)


def draw_post_attn_gain(key, part):
    magnitude, direction = profile(key)
    jitter = jax.random.uniform(jax.random.fold_in(key, 41), (D,), dtype=jnp.float32, minval=0.8, maxval=1.2)
    return (0.35 + 0.45 * magnitude * jitter).astype(jnp.float32)


def draw_post_ffw_gain(key, part):
    magnitude, direction = profile(key)
    jitter = jax.random.uniform(jax.random.fold_in(key, 42), (D,), dtype=jnp.float32, minval=0.8, maxval=1.2)
    return (0.35 + 0.45 * magnitude * jitter).astype(jnp.float32)


def draw_output_weight(key, part):
    magnitude, direction = profile(key)
    rough_key = jax.random.fold_in(key, 51)
    shared_key = jax.random.fold_in(key, 52)
    rough = clipped_normal(rough_key, (H * HD, D), 4.0)
    shared = clipped_normal(shared_key, (1, D), 3.0)
    column = (magnitude / PROFILE_RMS)[None, :]
    return (column * (rough + shared) * (2 * H * HD) ** (-0.5)).astype(jnp.bfloat16)


def unit_pair(key):
    first = clipped_normal(jax.random.fold_in(key, 61), (D, FF), 4.0)
    second = clipped_normal(jax.random.fold_in(key, 62), (D, FF), 4.0)
    return (first, second)


def draw_gate_weight(key, part):
    first, second = unit_pair(key)
    return (first * D ** (-0.5)).astype(jnp.bfloat16)


def draw_up_weight(key, part):
    first, second = unit_pair(key)
    return ((0.7 * first + 0.714 * second) * D ** (-0.5)).astype(jnp.bfloat16)


def draw_down_weight(key, part):
    magnitude, direction = profile(key)
    rough = clipped_normal(jax.random.fold_in(key, 71), (FF, D), 4.0)
    return ((rough + 2.0 * FF ** (-0.5) * direction[None, :]) * FF ** (-0.5)).astype(jnp.bfloat16)


def draw_embedding(key, part):
    magnitude, direction = profile(key)
    rough_key = jax.random.fold_in(key, 81)
    lean_key = jax.random.fold_in(key, 82)
    rough = clipped_normal(rough_key, (VOCAB, D), 4.0)
    lean = 0.15 * clipped_normal(lean_key, (VOCAB, 1), 4.0)
    return ((rough + lean * direction[None, :]) * D ** (-0.5)).astype(jnp.bfloat16)


def block_scale(key, dims, pieces, least, largest):
    def one(dim, blocks):
        draws = jax.random.uniform(jax.random.fold_in(jax.random.fold_in(key, 6), dim), (blocks,), jnp.float32, least / len(pieces), largest / len(pieces))
        return jnp.repeat(jnp.exp(draws), dims[dim] // blocks).reshape((-1,) + (1,) * (len(dims) - dim - 1))

    loudness = one(*pieces[0])
    for cut in pieces[1:]:
        loudness = loudness * one(*cut)
    return loudness


def centred(own_key, dims, scale, bound, shards=(), kind=jnp.bfloat16):
    loudness = block_scale(own_key, dims, shards, -0.22, 0.18) if shards else 1.0
    array = jax.random.normal(own_key, dims, jnp.float32) * scale * loudness
    return jnp.minimum(jnp.maximum(array, -bound), bound).astype(kind)


def setup_inputs(seed: int = 0) -> dict:
    splits = jax.random.split(jax.random.key(seed), 23)
    hidden = draw_hidden(jax.random.fold_in(splits[22], 71), 0)
    lengths = draw_lengths(jax.random.fold_in(splits[22], 71), 0)
    slot_owner = jax.vmap(lambda own: jax.random.permutation(own, R))(jax.random.split(splits[2], 2)).reshape((2, R)).astype(jnp.int32)
    allowed_ids = draw_allowed_ids(jax.random.fold_in(splits[22], 71), 0)
    guidance = jnp.clip(jax.random.uniform(splits[4], (R,), jnp.float32, 1.0, 4.0), 1.0, 4.0)
    pre_attn_gain = jnp.clip(1.0 + 0.18 * jax.random.normal(splits[5], (D,), jnp.float32), 0.1, 1.9)
    post_attn_gain = draw_post_attn_gain(jax.random.fold_in(splits[22], 71), 0)
    pre_ffw_gain = jnp.clip(1.0 + 0.18 * jax.random.normal(splits[7], (D,), jnp.float32), 0.1, 1.9)
    post_ffw_gain = draw_post_ffw_gain(jax.random.fold_in(splits[22], 71), 0)
    final_gain = jnp.clip(1.0 + 0.18 * jax.random.normal(splits[9], (D,), jnp.float32), 0.1, 1.9)
    query_weight = centred(splits[10], (D, H * HD), D ** -0.5, 0.09375, ((0, 32), (1, 4)))
    key_weight = centred(splits[11], (D, KVH * HD), D ** -0.5, 0.09375, ((0, 32), (1, 4)))
    value_weight = centred(splits[12], (D, KVH * HD), D ** -0.5, 0.09375, ((0, 32), (1, 4)))
    output_weight = draw_output_weight(jax.random.fold_in(splits[22], 71), 0)
    gate_weight = draw_gate_weight(jax.random.fold_in(splits[22], 71), 0)
    up_weight = draw_up_weight(jax.random.fold_in(splits[22], 71), 0)
    down_weight = draw_down_weight(jax.random.fold_in(splits[22], 71), 0)
    embedding = draw_embedding(jax.random.fold_in(splits[22], 71), 0)
    cond_keys = centred(splits[18], (R, CAP, KVH * HD), 1.0, 6.0, ((1, 32), (2, 4)))
    cond_values = centred(splits[19], (R, CAP, KVH * HD), 1.0, 6.0, ((1, 32), (2, 4)))
    uncond_keys = centred(splits[20], (R, UCAP, KVH * HD), 1.0, 6.0, ((1, 32), (2, 4)))
    uncond_values = centred(splits[21], (R, UCAP, KVH * HD), 1.0, 6.0, ((1, 32), (2, 4)))
    return {"hidden": hidden, "lengths": lengths, "slot_owner": slot_owner, "allowed_ids": allowed_ids, "guidance": guidance, "pre_attn_gain": pre_attn_gain, "post_attn_gain": post_attn_gain, "pre_ffw_gain": pre_ffw_gain, "post_ffw_gain": post_ffw_gain, "final_gain": final_gain, "query_weight": query_weight, "key_weight": key_weight, "value_weight": value_weight, "output_weight": output_weight, "gate_weight": gate_weight, "up_weight": up_weight, "down_weight": down_weight, "embedding": embedding, "cond_keys": cond_keys, "cond_values": cond_values, "uncond_keys": uncond_keys, "uncond_values": uncond_values}


EPS = 1e-06
ATTN_CAP = 50.0
LOGIT_CAP = 30.0
THETA = 10000.0

def rotary(values, position):
    half_size = values.shape[-1] // 2
    frequency = THETA ** (-2.0 * jnp.arange(half_size, dtype=jnp.float32) / values.shape[-1])
    angles = position[:, None, None] * frequency
    first_half = values[..., :half_size]
    second_half = values[..., half_size:]
    cosine = jnp.cos(angles)
    sine_part = jnp.sin(angles)
    return jnp.concatenate([first_half * cosine - second_half * sine_part, second_half * cosine + first_half * sine_part], axis=-1)

def reference(hidden, lengths, slot_owner, allowed_ids, guidance, pre_attn_gain, post_attn_gain, pre_ffw_gain, post_ffw_gain, final_gain, query_weight, key_weight, value_weight, output_weight, gate_weight, up_weight, down_weight, embedding, cond_keys, cond_values, uncond_keys, uncond_values):
    streams = hidden.astype(jnp.float32).reshape(2 * R, D)
    square_sum = lax.optimization_barrier(jnp.sum(streams * streams, axis=-1))
    row_scale = lax.rsqrt(square_sum / D + EPS)[:, None]
    normed = (streams * pre_attn_gain).astype(jnp.bfloat16)
    position = lengths.astype(jnp.float32).reshape(2 * R)
    query_full = jnp.dot(normed, query_weight, preferred_element_type=jnp.float32) * row_scale
    key_full = jnp.dot(normed, key_weight, preferred_element_type=jnp.float32) * row_scale
    value_full = jnp.dot(normed, value_weight, preferred_element_type=jnp.float32) * row_scale
    queries = (rotary(query_full.reshape(2 * R, H, HD), position) * (D // H) ** (-0.5)).astype(jnp.bfloat16)
    new_keys = rotary(key_full.reshape(2 * R, KVH, HD), position).astype(jnp.bfloat16)
    new_values = value_full.reshape(2 * R, KVH, HD).astype(jnp.bfloat16)
    inverse = jnp.argsort(slot_owner, axis=1).astype(jnp.int32)
    group_size = H // KVH

    def make_stream(kind, key_cache, value_cache):
        span = key_cache.shape[1]

        def one_stream(request):
            index = kind * R + request
            slot = inverse[kind, request]
            key_rows = key_cache[slot].astype(jnp.float32).reshape(span, KVH, HD)
            value_rows = value_cache[slot].astype(jnp.float32).reshape(span, KVH, HD)
            query = queries[index].astype(jnp.float32).reshape(KVH, group_size, HD)
            scores = jnp.einsum('kgd,tkd->kgt', query, key_rows)
            visible = jnp.arange(span, dtype=jnp.int32) < lengths[kind, request]
            probs = jnp.where(visible[None, None, :], jnp.exp(ATTN_CAP * jnp.tanh(scores / ATTN_CAP)), 0.0)
            rounded = lax.optimization_barrier(probs.astype(jnp.bfloat16)).astype(jnp.float32)
            numer = jnp.einsum('kgt,tkd->kgd', rounded, value_rows)
            own_score = jnp.einsum('kgd,kd->kg', query, new_keys[index].astype(jnp.float32))
            own_prob = jnp.exp(ATTN_CAP * jnp.tanh(own_score / ATTN_CAP))
            own_round = lax.optimization_barrier(own_prob.astype(jnp.bfloat16)).astype(jnp.float32)
            numer = numer + own_round[:, :, None] * new_values[index].astype(jnp.float32)[:, None, :]
            denom = lax.optimization_barrier(jnp.sum(probs, axis=-1)) + own_prob
            return (numer / denom[:, :, None]).astype(jnp.bfloat16).reshape(H * HD)
        return one_stream
    cond_att = lax.map(make_stream(0, cond_keys, cond_values), jnp.arange(R, dtype=jnp.int32))
    uncond_att = lax.map(make_stream(1, uncond_keys, uncond_values), jnp.arange(R, dtype=jnp.int32))
    attended = jnp.concatenate([cond_att, uncond_att], axis=0)
    projected = jnp.dot(attended, output_weight, preferred_element_type=jnp.float32)
    out_scale = lax.rsqrt(lax.optimization_barrier(jnp.sum(projected * projected, axis=-1)) / D + EPS)[:, None]
    middle = streams + projected * out_scale * post_attn_gain
    mid_scale = lax.rsqrt(lax.optimization_barrier(jnp.sum(middle * middle, axis=-1)) / D + EPS)[:, None]
    ffw_in = (middle * pre_ffw_gain).astype(jnp.bfloat16)
    gate = jnp.dot(ffw_in, gate_weight, preferred_element_type=jnp.float32) * mid_scale
    upward = jnp.dot(ffw_in, up_weight, preferred_element_type=jnp.float32) * mid_scale
    activ = (jax.nn.gelu(gate, approximate=True) * upward).astype(jnp.bfloat16)
    ffw_out = jnp.dot(activ, down_weight, preferred_element_type=jnp.float32)
    ffw_scale = lax.rsqrt(lax.optimization_barrier(jnp.sum(ffw_out * ffw_out, axis=-1)) / D + EPS)[:, None]
    last = middle + ffw_out * ffw_scale * post_ffw_gain
    final_scale = lax.rsqrt(lax.optimization_barrier(jnp.sum(last * last, axis=-1)) / D + EPS)[:, None]
    final_rows = (last * final_gain).astype(jnp.bfloat16)
    full_logits = jnp.dot(final_rows, embedding.T, preferred_element_type=jnp.float32)
    chosen = jnp.take(full_logits, allowed_ids, axis=1)
    logits = (LOGIT_CAP * jnp.tanh(chosen * final_scale / LOGIT_CAP)).reshape(2, R, ALLOWED)
    return logits[1] + guidance[:, None] * (logits[0] - logits[1])
```

```python
import jax
import jax.numpy as jnp
from jax import lax
from jax.experimental import pallas as pl
from jax.experimental.pallas import tpu as pltpu
from jax.sharding import PartitionSpec as P

D = 4608
H = 32
HD = 128
EPS = 1e-06
ATTN_CAP = 50.0
LOGIT_CAP = 30.0
THETA = 10000.0
MESH = pl.DeviceIdType.MESH
F32 = jnp.float32
BF16 = jnp.bfloat16
NG, NKV, NS = 2, 4, 16
NP = NG * NS
WL = D // NP
FFL = 9216
FB = 256
EXTRA = 8
ROWS = 2048
HALF = D // 2
PICK = 1024


def iota(shape, dim):
    return lax.broadcasted_iota(jnp.int32, shape, dim)


def column_to_row(col):
    n = col.shape[0]
    spread = jnp.where(iota((n, 128), 0) == iota((n, 128), 1), jnp.broadcast_to(col, (n, 128)), 0.0)
    return jnp.sum(spread, axis=0, keepdims=True)


def row_to_column(row, n, first=0):
    lanes = iota((n, 128), 1)
    picked = jnp.where(lanes == iota((n, 128), 0) + first, jnp.broadcast_to(row, (n, 128)), 0.0)
    return jnp.sum(picked, axis=1, keepdims=True)


def nt_dot(a, b):
    return lax.dot_general(a, b, (((1,), (1,)), ((), ())), preferred_element_type=F32)


def nn_dot(a, b):
    return jnp.dot(a, b, preferred_element_type=F32)


def one_hot(mask):
    return jnp.where(mask, 1.0, 0.0).astype(BF16)


def step_kernel(
    lengths, owner, guidance, hidden, ids, cosine, sine, gains,
    qw_h, kw_h, vw_h, ow_h, gw_h, uw_h, dw_h, emb_h, ck_h, cv_h, uk_h, uv_h,
    out_ref,
    w_qkv, w_o, w_g, w_u, w_d, emb, ck, cv, uk, uv,
    pick, qs, ks, vs, rows_f,
    s1, r1, b2, s3, r3, b4, b5, b6, bm, b7, s8, r8, s9, r9, act, b12, b13, b14, s16, r16, s15, r15,
    load_sem, send_sem, recv_sem,
):
    g = lax.axis_index("guide")
    kv = lax.axis_index("kv")
    s = lax.axis_index("seq")
    z = lax.div(s, 4)
    x = lax.rem(s, 4)
    me = g * NS + s

    loads = [
        pltpu.make_async_copy(src, dst, load_sem.at[i])
        for i, (src, dst) in enumerate(
            [
                (qw_h, w_qkv.at[:, pl.ds(0, 1024)]),
                (kw_h, w_qkv.at[:, pl.ds(1024, 512)]),
                (vw_h, w_qkv.at[:, pl.ds(1536, 512)]),
                (ck_h, ck),
                (uk_h, uk),
                (cv_h, cv),
                (uv_h, uv),
                (ow_h, w_o),
                (gw_h, w_g),
                (uw_h, w_u),
                (dw_h, w_d),
                (emb_h, emb),
            ]
        )
    ]
    for load in loads:
        load.start()

    def peer(off):
        g2 = lax.rem(g + lax.div(off, 16), 2)
        z2 = lax.rem(z + lax.div(lax.rem(off, 16), 4), 4)
        x2 = lax.rem(x + lax.rem(off, 4), 4)
        return g2, z2 * 4 + x2

    def to_plane(body, count=NP):
        def one(off, carry):
            g2, s2 = peer(off)
            body(g2, s2)
            return carry

        lax.fori_loop(1, count, one, 0)

    def to_kv(body):
        for off in range(1, NKV):
            body(lax.rem(kv + off, NKV))

    def send(src, dst, i, device):
        pltpu.make_async_remote_copy(
            src_ref=src, dst_ref=dst, send_sem=send_sem.at[i], recv_sem=recv_sem.at[i],
            device_id=device, device_id_type=MESH,
        ).start()

    def whole(ref, i):
        return pltpu.make_async_remote_copy(
            src_ref=ref, dst_ref=ref, send_sem=send_sem.at[i], recv_sem=recv_sem.at[i],
            device_id={"guide": lax.rem(g + 1, 2)}, device_id_type=MESH,
        )

    barrier = pltpu.get_barrier_semaphore()
    to_plane(lambda g2, s2: pl.semaphore_signal(
        barrier, inc=1, device_id={"guide": g2, "seq": s2}, device_id_type=MESH))
    to_kv(lambda k2: pl.semaphore_signal(barrier, inc=1, device_id={"kv": k2}, device_id_type=MESH))

    x_in = hidden[...].astype(F32).reshape(16, WL)
    gain = gains[...]
    normed = (x_in * gain[0:1, :]).astype(BF16)
    x_sq = column_to_row(jnp.sum(x_in * x_in, axis=-1, keepdims=True))
    for i in range(3):
        loads[i].wait()
    part = nn_dot(normed, w_qkv[...])
    for j in range(NS):
        for k in range(NG):
            s1[k * NS + j, 0:8, :] = part[k * 8:(k + 1) * 8, j * 128:(j + 1) * 128]
            s1[k * NS + j, 8:9, :] = x_sq
    r1[me] = s1[me]
    pl.semaphore_wait(barrier, NP - 1 + NKV - 1)
    to_plane(lambda g2, s2: send(
        s1.at[g2 * NS + s2], r1.at[me], 0, {"guide": g2, "seq": s2}))

    first_row = (kv * NS + s) * ROWS

    def pick_rows(i, carry):
        base = pl.multiple_of(i * 256, 256)
        v = iota((256, 128), 0) + (first_row + base)
        for c in range(PICK // 128):
            pick[pl.ds(base, 256), c * 128:(c + 1) * 128] = one_hot(v == ids[c:c + 1, :])
        return carry

    lax.fori_loop(0, ROWS // 256, pick_rows, 0)

    whole(r1.at[pl.ds(0, NP - 1)], 0).wait_recv()
    total = jnp.sum(r1[...], axis=0)
    scale = lax.rsqrt(row_to_column(total[8:9, :], 8, 8 * g) / D + EPS)
    y = total[0:8, :] * scale
    turned = y * cosine[g] + pltpu.roll(y, 64, 1) * sine[g]
    y = jnp.where(s < 12, turned, y)
    y = jnp.where(s < 8, y * (D // H) ** (-0.5), y)
    b2[me] = y.astype(BF16).astype(F32)
    to_plane(lambda g2, s2: send(b2.at[me], b2.at[me], 1, {"guide": g2, "seq": s2}))

    picks = []
    r_ = iota((64, 128), 0)
    c_ = iota((64, 128), 1)
    for k in range(NG):
        held = jnp.zeros((64, 128), jnp.int32)
        for j in range(8):
            held = jnp.where(lax.div(r_, 8) == j, owner[k, j], held)
        same = lax.rem(c_, 8) == held
        head = lax.rem(r_, 8)
        blk = lax.div(c_, 8)
        picks.append((
            one_hot(same & (blk == head)),
            one_hot(same & (blk == 8 + lax.div(head, 2))),
            one_hot(same & (blk == 12 + lax.div(head, 2))),
        ))
    block = me
    limits = []
    for k, span in ((0, 256), (1, 64)):
        limit = jnp.zeros((64, span), jnp.int32)
        row = lax.div(iota((64, span), 0), 8)
        for j in range(8):
            limit = jnp.where(row == j, lengths[k, owner[k, j]], limit)
        limits.append(iota((64, span), 1) + block * span < limit)

    for i in range(3, 7):
        loads[i].wait()
    whole(b2.at[pl.ds(0, NP - 1)], 1).wait_recv()
    gathered = b2[...].reshape(NG, 128, 128).astype(BF16)
    lane_head = lax.div(lax.rem(iota((64, 128), 0), 8), 2)
    for k, span, keys, values in ((0, 256, ck, cv), (1, 64, uk, uv)):
        q = nn_dot(picks[k][0], gathered[k])
        for j in range(8):
            qs[k * 8 + j] = q[j * 8:(j + 1) * 8, :]
        wide = [jnp.where(lane_head == b, q, 0.0) for b in range(4)]
        scores = []
        for j in range(8):
            qj = jnp.concatenate([w[j * 8:(j + 1) * 8, :] for w in wide], axis=1).astype(BF16)
            scores.append(nt_dot(qj, keys[j]))
        score = jnp.concatenate(scores, axis=0)
        prob = jnp.where(limits[k], jnp.exp(ATTN_CAP * jnp.tanh(score / ATTN_CAP)), 0.0)
        denom = jnp.sum(prob, axis=1, keepdims=True)
        for j in range(8):
            pj = prob[j * 8:(j + 1) * 8, :].astype(BF16)
            full = nn_dot(pj, values[j])
            mine = jnp.zeros((8, 128), F32)
            for b in range(4):
                mine = jnp.where(lane_head[0:8, :] == b, full[:, b * 128:(b + 1) * 128], mine)
            s3[k * 8 + j, 0:8, :] = mine
            s3[k * 8 + j, 8:9, :] = column_to_row(denom[j * 8:(j + 1) * 8, :])

    tile_guide = lax.rem(s, 2)
    holds_tile = g == tile_guide

    def send_tile(off, carry):
        i = lax.rem(s + off, NS)
        send(s3.at[i], r3.at[me], 2, {"guide": lax.rem(i, 2), "seq": i})
        return carry

    lax.fori_loop(1, NS, send_tile, 0)

    @pl.when(jnp.logical_not(holds_tile))
    def _():
        send(s3.at[s], r3.at[me], 2, {"guide": tile_guide, "seq": s})

    for k in range(NG):
        kx = nn_dot(picks[k][1], gathered[k])
        vx = nn_dot(picks[k][2], gathered[k])
        for j in range(8):
            ks[k * 8 + j] = kx[j * 8:(j + 1) * 8, :]
            vs[k * 8 + j] = vx[j * 8:(j + 1) * 8, :]

    @pl.when(holds_tile)
    def _():
        r3[me] = s3[s]
        own = jnp.exp(ATTN_CAP * jnp.tanh(jnp.sum(qs[s] * ks[s], axis=1, keepdims=True) / ATTN_CAP))
        whole(r3.at[pl.ds(0, NP - 1)], 2).wait_recv()
        sums = jnp.sum(r3[...], axis=0)
        numer = sums[0:8, :] + own.astype(BF16).astype(F32) * vs[s]
        den = row_to_column(sums[8:9, :], 8) + own
        b4[s] = (numer / den).astype(BF16).astype(F32)
        to_plane(lambda g2, s2: send(b4.at[s], b4.at[s], 3, {"guide": g2, "seq": s2}))

    r_ = iota((128, 128), 0)
    c_ = iota((128, 128), 1)
    held = jnp.zeros((128, 128), jnp.int32)
    for i in range(16):
        held = jnp.where(lax.div(c_, 8) == i, owner[i // 8, i % 8], held)
    back = one_hot(
        (lax.div(r_, 16) == lax.rem(c_, 8))
        & (lax.rem(lax.div(r_, 8), 2) == lax.div(c_, 64))
        & (lax.rem(r_, 8) == held)
    )
    loads[7].wait()

    @pl.when(holds_tile)
    def _():
        whole(b4.at[pl.ds(0, NS - 1)], 3).wait_recv()

    @pl.when(jnp.logical_not(holds_tile))
    def _():
        whole(b4, 3).wait_recv()

    att = nn_dot(back, b4[...].reshape(128, 128).astype(BF16))
    att = jnp.concatenate([att[h * 16:(h + 1) * 16, :] for h in range(8)], axis=1).astype(BF16)
    b5[kv] = nn_dot(att, w_o[...])
    to_kv(lambda k2: send(b5.at[kv], b5.at[kv], 4, {"kv": k2}))
    whole(b5.at[pl.ds(0, NKV - 1)], 4).wait_recv()
    projected = (b5[0] + b5[1]) + (b5[2] + b5[3])
    b6[me] = column_to_row(jnp.sum(projected * projected, axis=-1, keepdims=True))
    to_plane(lambda g2, s2: send(b6.at[me], b6.at[me], 5, {"guide": g2, "seq": s2}))
    whole(b6.at[pl.ds(0, NP - 1)], 5).wait_recv()
    branch_sq = row_to_column(jnp.sum(b6[...], axis=0), 16)
    out_scale = lax.rsqrt(branch_sq / D + EPS)
    middle = x_in + projected * out_scale * gain[1:2, :]
    b7[me] = column_to_row(jnp.sum(middle * middle, axis=-1, keepdims=True))
    ffw_in = (middle * gain[2:3, :]).astype(BF16)

    loads[8].wait()
    loads[9].wait()

    def tile(g2, s2):
        r = g2 * NS + s2
        cols = pl.ds(pl.multiple_of(r * FB, FB), FB)
        s8[r, :, 0:FB] = nn_dot(ffw_in, w_g[:, cols]).astype(BF16)
        s8[r, :, FB:2 * FB] = nn_dot(ffw_in, w_u[:, cols]).astype(BF16)

    def tile_out(g2, s2):
        tile(g2, s2)
        send(s8.at[g2 * NS + s2], r8.at[me], 6, {"guide": g2, "seq": s2})

    tail = NP * FB
    g_tail = nn_dot(ffw_in, w_g[:, tail:FFL]).astype(BF16)
    u_tail = nn_dot(ffw_in, w_u[:, tail:FFL]).astype(BF16)
    for e in range(EXTRA):
        s9[e, :, 0:128] = g_tail[:, e * 128:(e + 1) * 128]
        s9[e, :, 128:256] = u_tail[:, e * 128:(e + 1) * 128]
    holds_extra = (g == 0) & (lax.rem(x, 2) == lax.rem(z, 2))
    extra = 2 * z + lax.div(x, 2)

    def send_extra(e, carry):
        z2 = lax.div(e, 2)
        s2 = 4 * z2 + 2 * lax.rem(e, 2) + lax.rem(z2, 2)

        @pl.when(jnp.logical_or(g != 0, s2 != s))
        def _():
            send(s9.at[e], r9.at[me], 7, {"guide": 0, "seq": s2})

        return carry

    lax.fori_loop(0, EXTRA, send_extra, 0)
    to_plane(tile_out)
    tile(g, s)
    r8[me] = s8[me]
    to_plane(lambda g2, s2: send(b7.at[me], b7.at[me], 8, {"guide": g2, "seq": s2}))
    bm[s, 0:16, :] = middle
    bm[s, 16:18, :] = gain[3:5, :]
    to_plane(lambda g2, s2: send(bm.at[s], bm.at[s], 9, {"seq": s2}), NS)

    whole(b7.at[pl.ds(0, NP - 1)], 8).wait_recv()
    ffw_scale = lax.rsqrt(row_to_column(jnp.sum(b7[...], axis=0), 16) / D + EPS)

    def activate(gate, up):
        gate = gate * ffw_scale
        return (jax.nn.gelu(gate, approximate=True) * (up * ffw_scale)).astype(BF16)

    whole(r8.at[pl.ds(0, NP - 1)], 6).wait_recv()
    sums = jnp.sum(r8[...].astype(F32), axis=0)
    mine = pl.ds(pl.multiple_of(me * FB, FB), FB)
    act[:, mine] = activate(sums[:, 0:FB], sums[:, FB:2 * FB])
    to_plane(lambda g2, s2: send(act.at[:, mine], act.at[:, mine], 10, {"guide": g2, "seq": s2}))

    @pl.when(holds_extra)
    def _():
        r9[me] = s9[extra]
        whole(r9.at[pl.ds(0, NP - 1)], 7).wait_recv()
        sums = jnp.sum(r9[...].astype(F32), axis=0)
        cols = pl.ds(pl.multiple_of(tail + extra * 128, 128), 128)
        act[:, cols] = activate(sums[:, 0:128], sums[:, 128:256])
        to_plane(lambda g2, s2: send(act.at[:, cols], act.at[:, cols], 11, {"guide": g2, "seq": s2}))

    loads[10].wait()
    whole(act.at[:, pl.ds(0, (NP - 1) * FB)], 10).wait_recv()

    @pl.when(holds_extra)
    def _():
        whole(act.at[:, pl.ds(0, (EXTRA - 1) * 128)], 11).wait_recv()

    @pl.when(jnp.logical_not(holds_extra))
    def _():
        whole(act.at[:, pl.ds(0, EXTRA * 128)], 11).wait_recv()

    b12[kv] = nn_dot(act[...], w_d[...])
    to_kv(lambda k2: send(b12.at[kv], b12.at[kv], 12, {"kv": k2}))
    whole(b12.at[pl.ds(0, NKV - 1)], 12).wait_recv()
    ffw_out = (b12[0] + b12[1]) + (b12[2] + b12[3])
    b14[s] = ffw_out
    b13[me] = column_to_row(jnp.sum(ffw_out * ffw_out, axis=-1, keepdims=True))
    to_plane(lambda g2, s2: send(b14.at[s], b14.at[s], 14, {"seq": s2}), NS)
    to_plane(lambda g2, s2: send(b13.at[me], b13.at[me], 13, {"guide": g2, "seq": s2}))

    loads[11].wait()
    whole(bm.at[pl.ds(0, NS - 1)], 9).wait_recv()
    whole(b13.at[pl.ds(0, NP - 1)], 13).wait_recv()
    branch_scale = lax.rsqrt(row_to_column(jnp.sum(b13[...], axis=0), 16) / D + EPS)
    whole(b14.at[pl.ds(0, NS - 1)], 14).wait_recv()
    last_sq = jnp.zeros((16, 1), F32)
    for t in range(NS):
        last = bm[t, 0:16, :] + b14[t] * branch_scale * bm[t, 16:17, :]
        last_sq = last_sq + jnp.sum(last * last, axis=-1, keepdims=True)
        rows_f[:, t * WL:(t + 1) * WL] = last * bm[t, 17:18, :]
    s15[...] = column_to_row(last_sq)
    other = {"guide": lax.rem(g + 1, 2)}
    send(s15, r15, 15, other)

    full = nt_dot(rows_f[...].astype(BF16), emb[...])
    high = full.astype(BF16)
    low = (full - high.astype(F32)).astype(BF16)
    logit = nn_dot(jnp.concatenate([high, low], axis=0), pick[...])
    logit = logit[0:16, :] + logit[16:32, :]
    lower = jnp.concatenate([logit[0:4, :], logit[8:12, :]], axis=0)
    upper = jnp.concatenate([logit[4:8, :], logit[12:16, :]], axis=0)
    s16[...] = jnp.where(g == 0, upper, lower)
    send(s16, r16, 16, other)
    keep = jnp.where(g == 0, lower, upper)
    whole(r15, 15).wait_recv()
    lanes = iota((8, 128), 1)
    rowi = iota((8, 128), 0)
    want = lax.div(rowi, 4) * 8 + 4 * g + lax.rem(rowi, 4)
    sq = jnp.sum(jnp.where(lanes == want, jnp.broadcast_to(s15[...] + r15[...], (8, 128)), 0.0),
                 axis=1, keepdims=True)
    final_scale = lax.rsqrt(sq / D + EPS)
    share = jnp.zeros((4, 1), F32)
    for i in range(4):
        share = jnp.where(iota((4, 1), 0) == i, guidance[4 * g + i], share)
    whole(r16, 16).wait_recv()
    capped = LOGIT_CAP * jnp.tanh((keep + r16[...]) * final_scale / LOGIT_CAP)
    out_ref[...] = capped[4:8, :] + share * (capped[0:4, :] - capped[4:8, :])

    whole(s1.at[pl.ds(0, NP - 1)], 0).wait_send()
    whole(b2.at[pl.ds(0, NP - 1)], 1).wait_send()

    @pl.when(holds_tile)
    def _():
        whole(s3.at[pl.ds(0, NS - 1)], 2).wait_send()
        for_out = s1.at[pl.ds(0, NP - 1), pl.ds(0, 8)]
        whole(for_out, 3).wait_send()

    @pl.when(jnp.logical_not(holds_tile))
    def _():
        whole(s3, 2).wait_send()

    whole(b5.at[pl.ds(0, NKV - 1)], 4).wait_send()
    whole(b6.at[pl.ds(0, NP - 1)], 5).wait_send()
    whole(s8.at[pl.ds(0, NP - 1)], 6).wait_send()

    @pl.when(holds_extra)
    def _():
        whole(s9.at[pl.ds(0, EXTRA - 1)], 7).wait_send()
        whole(act.at[:, pl.ds(0, (NP - 1) * 128)], 11).wait_send()

    @pl.when(jnp.logical_not(holds_extra))
    def _():
        whole(s9, 7).wait_send()

    whole(b7.at[pl.ds(0, NP - 1)], 8).wait_send()
    whole(bm.at[pl.ds(0, NS - 1)], 9).wait_send()
    whole(act.at[:, pl.ds(0, (NP - 1) * FB)], 10).wait_send()
    whole(b12.at[pl.ds(0, NKV - 1)], 12).wait_send()
    whole(b13.at[pl.ds(0, NP - 1)], 13).wait_send()
    whole(b14.at[pl.ds(0, NS - 1)], 14).wait_send()
    whole(s15, 15).wait_send()
    whole(s16, 16).wait_send()


def on_device(
    hidden, lengths, slot_owner, allowed_ids, guidance,
    pre_attn_gain, post_attn_gain, pre_ffw_gain, post_ffw_gain, final_gain,
    query_weight, key_weight, value_weight, output_weight,
    gate_weight, up_weight, down_weight, embedding,
    cond_keys, cond_values, uncond_keys, uncond_values,
):
    position = lengths.astype(F32)
    frequency = THETA ** (-2.0 * jnp.arange(HD // 2, dtype=F32) / HD)
    angles = position[:, :, None] * frequency
    cosine = jnp.cos(angles)
    sine = jnp.sin(angles)
    cosine = jnp.concatenate([cosine, cosine], axis=-1)
    sine = jnp.concatenate([-sine, sine], axis=-1)
    gains = jnp.stack([pre_attn_gain, post_attn_gain, pre_ffw_gain, post_ffw_gain, final_gain])
    smem = pl.BlockSpec(memory_space=pltpu.SMEM)
    vmem = pl.BlockSpec(memory_space=pltpu.VMEM)
    hbm = pl.BlockSpec(memory_space=pl.ANY)
    return pl.pallas_call(
        step_kernel,
        out_shape=jax.ShapeDtypeStruct((4, PICK), F32),
        in_specs=[smem] * 3 + [vmem] * 5 + [hbm] * 12,
        out_specs=vmem,
        scratch_shapes=[
            pltpu.VMEM((WL, 2048), BF16),
            pltpu.VMEM((1024, WL), BF16),
            pltpu.VMEM((WL, FFL), BF16),
            pltpu.VMEM((WL, FFL), BF16),
            pltpu.VMEM((FFL, WL), BF16),
            pltpu.VMEM((ROWS, HALF), BF16),
            pltpu.VMEM((8, 256, 512), BF16),
            pltpu.VMEM((8, 256, 512), BF16),
            pltpu.VMEM((8, 64, 512), BF16),
            pltpu.VMEM((8, 64, 512), BF16),
            pltpu.VMEM((ROWS, PICK), BF16),
            pltpu.VMEM((16, 8, 128), F32),
            pltpu.VMEM((16, 8, 128), F32),
            pltpu.VMEM((16, 8, 128), F32),
            pltpu.VMEM((16, HALF), F32),
            pltpu.VMEM((NP, 9, 128), F32),
            pltpu.VMEM((NP, 9, 128), F32),
            pltpu.VMEM((NP, 8, 128), F32),
            pltpu.VMEM((16, 9, 128), F32),
            pltpu.VMEM((NP, 9, 128), F32),
            pltpu.VMEM((16, 8, 128), F32),
            pltpu.VMEM((NKV, 16, WL), F32),
            pltpu.VMEM((NP, 1, 128), F32),
            pltpu.VMEM((NS, 18, WL), F32),
            pltpu.VMEM((NP, 1, 128), F32),
            pltpu.VMEM((NP, 16, 2 * FB), BF16),
            pltpu.VMEM((NP, 16, 2 * FB), BF16),
            pltpu.VMEM((EXTRA, 16, 256), BF16),
            pltpu.VMEM((NP, 16, 256), BF16),
            pltpu.VMEM((16, FFL), BF16),
            pltpu.VMEM((NKV, 16, WL), F32),
            pltpu.VMEM((NP, 1, 128), F32),
            pltpu.VMEM((NS, 16, WL), F32),
            pltpu.VMEM((8, PICK), F32),
            pltpu.VMEM((8, PICK), F32),
            pltpu.VMEM((1, 128), F32),
            pltpu.VMEM((1, 128), F32),
            pltpu.SemaphoreType.DMA((12,)),
            pltpu.SemaphoreType.DMA((17,)),
            pltpu.SemaphoreType.DMA((17,)),
        ],
        compiler_params=pltpu.CompilerParams(
            collective_id=0, has_side_effects=True, vmem_limit_bytes=60 * 1024 * 1024
        ),
        name="decode_step",
    )(
        lengths, slot_owner, guidance, hidden, allowed_ids.reshape(8, 128), cosine, sine, gains,
        query_weight, key_weight, value_weight, output_weight, gate_weight, up_weight, down_weight,
        embedding, cond_keys, cond_values, uncond_keys, uncond_values,
    )


def solution(mesh):
    return jax.shard_map(
        on_device,
        mesh=mesh,
        in_specs=(
            P(None, None, ("guide", "seq")),
            P(),
            P(),
            P(("kv", "seq")),
            P(),
            P(("guide", "seq")),
            P(("guide", "seq")),
            P(("guide", "seq")),
            P(("guide", "seq")),
            P(("guide", "seq")),
            P(("guide", "seq"), "kv"),
            P(("guide", "seq"), "kv"),
            P(("guide", "seq"), "kv"),
            P("kv", ("guide", "seq")),
            P(("guide", "seq"), "kv"),
            P(("guide", "seq"), "kv"),
            P("kv", ("guide", "seq")),
            P(("kv", "seq"), "guide"),
            P(None, ("guide", "seq"), "kv"),
            P(None, ("guide", "seq"), "kv"),
            P(None, ("guide", "seq"), "kv"),
            P(None, ("guide", "seq"), "kv"),
        ),
        out_specs=P("guide", ("kv", "seq")),
        check_vma=False,
    )
```

```python
import functools

import jax
import jax.numpy as jnp
import numpy as np
from jax import lax
from jax.experimental import pallas as pl
from jax.experimental.pallas import tpu as pltpu
from jax.sharding import PartitionSpec as P

D = 4608
H = 32
HD = 128
EPS = 1e-06
ATTN_CAP = 50.0
LOGIT_CAP = 30.0
THETA = 10000.0
MESH = pl.DeviceIdType.MESH
F32 = jnp.float32
BF16 = jnp.bfloat16
NG, NKV, NS = 2, 4, 16
NP = NG * NS
WL = D // NP
FFL = 9216
FB = 256
EXTRA = 8
ROWS = 2048
HALF = D // 2
PICK = 1024


def iota(shape, dim):
    return lax.broadcasted_iota(jnp.int32, shape, dim)


def column_to_row(col):
    n = col.shape[0]
    spread = jnp.where(iota((n, 128), 0) == iota((n, 128), 1), jnp.broadcast_to(col, (n, 128)), 0.0)
    return jnp.sum(spread, axis=0, keepdims=True)


def row_to_column(row, n, first=0):
    lanes = iota((n, 128), 1)
    picked = jnp.where(lanes == iota((n, 128), 0) + first, jnp.broadcast_to(row, (n, 128)), 0.0)
    return jnp.sum(picked, axis=1, keepdims=True)


def nt_dot(a, b):
    return lax.dot_general(a, b, (((1,), (1,)), ((), ())), preferred_element_type=F32)


def nn_dot(a, b):
    return jnp.dot(a, b, preferred_element_type=F32)


def one_hot(mask):
    return jnp.where(mask, 1.0, 0.0).astype(BF16)


def step_kernel(
    lengths, owner, guidance, hidden, ids, freq, gain0, gain1, gain2, gain3, gain4,
    qw_h, kw_h, vw_h, ow_h, gw_h, uw_h, dw_h, emb_h, ck_h, cv_h, uk_h, uv_h,
    base_ref, lift_ref,
    w_qkv, w_o, w_g, w_u, w_d, emb, ck, cv, uk, uv,
    pick, table, qs, ks, vs, rows_f,
    s1, r1, b2, s3, r3, b4, b5, b6, bm, act, b12, b13, b14, s16, r16, s15, r15,
    pa, qa, ka, sa, ra, ta, ua, va, wa, xa, pb, qb, kb, sb, rb, tb, ub, vb, wb, xb,
    load_sem, send_sem, recv_sem,
):
    g = lax.axis_index("guide")
    kv = lax.axis_index("kv")
    s = lax.axis_index("seq")
    z = lax.div(s, 4)
    x = lax.rem(s, 4)
    me = g * NS + s

    loads = [
        pltpu.make_async_copy(src, dst, load_sem.at[i])
        for i, (src, dst) in enumerate(
            [
                (qw_h, w_qkv.at[:, pl.ds(0, 1024)]),
                (kw_h, w_qkv.at[:, pl.ds(1024, 512)]),
                (vw_h, w_qkv.at[:, pl.ds(1536, 512)]),
                (ck_h, ck),
                (uk_h, uk),
                (cv_h, cv),
                (uv_h, uv),
                (ow_h, w_o),
                (gw_h, w_g),
                (uw_h, w_u),
                (dw_h, w_d),
                (emb_h, emb),
            ]
        )
    ]
    for load in loads[0:3]:
        load.start()

    def peer(off):
        g2 = lax.rem(g + lax.div(off, 16), 2)
        z2 = lax.rem(z + lax.div(lax.rem(off, 16), 4), 4)
        x2 = lax.rem(x + lax.rem(off, 4), 4)
        return g2, z2 * 4 + x2

    def to_plane(body, count=NP):
        def one(off, carry):
            g2, s2 = peer(off)
            body(g2, s2)
            return carry

        lax.fori_loop(1, count, one, 0)

    def to_kv(body):
        for off in range(1, NKV):
            body(lax.rem(kv + off, NKV))

    def send(src, dst, i, device):
        pltpu.make_async_remote_copy(
            src_ref=src, dst_ref=dst, send_sem=send_sem.at[i], recv_sem=recv_sem.at[i],
            device_id=device, device_id_type=MESH,
        ).start()

    def whole(ref, i):
        return pltpu.make_async_remote_copy(
            src_ref=ref, dst_ref=ref, send_sem=send_sem.at[i], recv_sem=recv_sem.at[i],
            device_id={"guide": lax.rem(g + 1, 2)}, device_id_type=MESH,
        )

    pending = []

    def finish():
        for ref, i, when in pending:
            if when is None:
                whole(ref, i).wait_send()
            else:
                pl.when(when)(functools.partial(lambda ref, i: whole(ref, i).wait_send(), ref, i))

    barrier = pltpu.get_barrier_semaphore()
    to_plane(lambda g2, s2: pl.semaphore_signal(
        barrier, inc=1, device_id={"guide": g2, "seq": s2}, device_id_type=MESH))
    to_kv(lambda k2: pl.semaphore_signal(barrier, inc=1, device_id={"kv": k2}, device_id_type=MESH))

    other = {"guide": lax.rem(g + 1, 2)}
    tail = NP * FB
    holds_extra = (lax.rem(x, 2) == lax.rem(z, 2)) & (lax.div(z, 2) == g)
    extra = 2 * z + lax.div(x, 2)
    set_a = (pa, qa, ka, sa, ra, ta, ua, va, wa, xa)
    set_b = (pb, qb, kb, sb, rb, tb, ub, vb, wb, xb)

    def ffw_product(rows, buffers, base):
        away, _, keep, _, _, tail_away, _, tail_keep, _, _ = buffers
        high = rows.astype(BF16)
        low = (rows - high.astype(F32)).astype(BF16)
        both = jnp.concatenate([high, low], axis=0)

        def product(weight, cols):
            wide = nn_dot(both, weight[:, cols])
            return wide[0:16, :] + wide[16:32, :]

        for whose, main, rest in ((1 - g, away, tail_away), (g, keep, tail_keep)):
            cols = pl.ds(pl.multiple_of(whose * (NS * FB), NS * FB), NS * FB)
            tail_cols = pl.ds(pl.multiple_of(tail + whose * 512, 512), 512)
            for at, weight in ((0, w_g), (1, w_u)):
                part = product(weight, cols).astype(main.dtype)
                for c in range(NS):
                    main[c, :, at * FB:(at + 1) * FB] = part[:, c * FB:(c + 1) * FB]
                part = product(weight, tail_cols).astype(rest.dtype)
                for c in range(4):
                    rest[c, :, at * 128:(at + 1) * 128] = part[:, c * 128:(c + 1) * 128]
            if main is away:
                send(away, buffers[1], base, other)
                send(tail_away, buffers[6], base + 1, other)
                pending.append((away, base, None))
                pending.append((tail_away, base + 1, None))

    def ffw_combine(buffers, base):
        _, came, keep, out, _, _, tail_came, tail_keep, tail_out, _ = buffers
        whole(came, base).wait_recv()
        whole(tail_came, base + 1).wait_recv()
        out[...] = (keep[...] + came[...].astype(F32)).astype(BF16)
        tail_out[...] = (tail_keep[...] + tail_came[...].astype(F32)).astype(BF16)

    def ffw_send(buffers, base):
        _, _, _, out, into, _, _, _, tail_out, tail_into = buffers

        def one(q, carry):
            z2 = 2 * g + lax.div(q, 2)
            s2 = 4 * z2 + 2 * lax.rem(q, 2) + lax.rem(z2, 2)

            @pl.when(s2 != s)
            def _():
                send(tail_out.at[q], tail_into.at[s], base + 1, {"seq": s2})

            return carry

        lax.fori_loop(0, 4, one, 0)
        to_plane(lambda g2, s2: send(out.at[s2], into.at[s], base, {"seq": s2}), NS)
        into[s] = out[s]
        pending.append((out.at[pl.ds(0, NS - 1)], base, None))
        pending.append((tail_out.at[pl.ds(0, 3)], base + 1, holds_extra))
        pending.append((tail_out, base + 1, jnp.logical_not(holds_extra)))

    x_in = hidden[...].astype(F32).reshape(16, WL)
    normed = (x_in * gain0[...]).astype(BF16)
    x_sq = column_to_row(jnp.sum(x_in * x_in, axis=-1, keepdims=True))
    for i in range(3):
        loads[i].wait()
    for load in loads[3:12]:
        load.start()
    part = nn_dot(normed, w_qkv[...])
    for j in range(NS):
        for k in range(NG):
            s1[k * NS + j, 0:8, :] = part[k * 8:(k + 1) * 8, j * 128:(j + 1) * 128]
            s1[k * NS + j, 8:9, :] = x_sq
    r1[me] = s1[me]

    first_row = (kv * NS + s) * ROWS

    def pick_rows(i, carry):
        base = pl.multiple_of(i * 256, 256)
        v = iota((256, 128), 0) + (first_row + base)
        for c in range(PICK // 128):
            pick[pl.ds(base, 256), c * 128:(c + 1) * 128] = one_hot(v == ids[c:c + 1, :])
        return carry

    def pick_table(first, count):
        def one(i, carry):
            cols = pl.ds(pl.multiple_of(i * 256, 256), 256)
            table[cols, :] = lax.dot_general(
                emb[:, cols], pick[...], (((0,), (0,)), ((), ())), preferred_element_type=F32
            ).astype(BF16)
            return carry

        lax.fori_loop(first, first + count, one, 0)

    turn_row = iota((8, 128), 0)
    position = jnp.zeros((8, 128), F32)
    for i in range(8):
        position = jnp.where(turn_row == i, lengths[g, i].astype(F32), position)
    angle = position * freq[...]
    cosine = jnp.cos(angle)
    sine = jnp.sin(angle)
    sine = jnp.where(iota((8, 128), 1) < 64, -sine, sine)
    pl.semaphore_wait(barrier, NP - 1 + NKV - 1)
    to_plane(lambda g2, s2: send(
        s1.at[g2 * NS + s2], r1.at[me], 0, {"guide": g2, "seq": s2}))
    pending.append((s1.at[pl.ds(0, NP - 1)], 0, None))

    lax.fori_loop(0, ROWS // 256, pick_rows, 0)
    whole(r1.at[pl.ds(0, NP - 1)], 0).wait_recv()
    total = jnp.sum(r1[...], axis=0)
    scale = lax.rsqrt(row_to_column(total[8:9, :], 8, 8 * g) / D + EPS)
    y = total[0:8, :] * scale
    turned = y * cosine + pltpu.roll(y, 64, 1) * sine
    y = jnp.where(s < 12, turned, y)
    y = jnp.where(s < 8, y * (D // H) ** (-0.5), y)
    b2[me] = y.astype(BF16).astype(F32)
    to_plane(lambda g2, s2: send(b2.at[me], b2.at[me], 1, {"guide": g2, "seq": s2}))
    pending.append((b2.at[pl.ds(0, NP - 1)], 1, None))

    picks = []
    r_ = iota((64, 128), 0)
    c_ = iota((64, 128), 1)
    for k in range(NG):
        held = jnp.zeros((64, 128), jnp.int32)
        for j in range(8):
            held = jnp.where(lax.div(r_, 8) == j, owner[k, j], held)
        same = lax.rem(c_, 8) == held
        head = lax.rem(r_, 8)
        blk = lax.div(c_, 8)
        picks.append((
            one_hot(same & (blk == head)),
            one_hot(same & (blk == 8 + lax.div(head, 2))),
            one_hot(same & (blk == 12 + lax.div(head, 2))),
        ))
    block = me
    limits = []
    for k, span in ((0, 256), (1, 64)):
        limit = jnp.zeros((64, span), jnp.int32)
        row = lax.div(iota((64, span), 0), 8)
        for j in range(8):
            limit = jnp.where(row == j, lengths[k, owner[k, j]], limit)
        limits.append(iota((64, span), 1) + block * span < limit)

    loads[8].wait()
    loads[9].wait()
    ffw_product(x_in * gain2[...], set_a, 6)
    for i in range(3, 7):
        loads[i].wait()
    whole(b2.at[pl.ds(0, NP - 1)], 1).wait_recv()
    gathered = b2[...].reshape(NG, 128, 128).astype(BF16)
    lane_head = lax.div(lax.rem(iota((64, 128), 0), 8), 2)
    for k, span, keys, values in ((0, 256, ck, cv), (1, 64, uk, uv)):
        q = nn_dot(picks[k][0], gathered[k])
        for j in range(8):
            qs[k * 8 + j] = q[j * 8:(j + 1) * 8, :]
        wide = [jnp.where(lane_head == b, q, 0.0) for b in range(4)]
        scores = []
        for j in range(8):
            qj = jnp.concatenate([w[j * 8:(j + 1) * 8, :] for w in wide], axis=1).astype(BF16)
            scores.append(nt_dot(qj, keys[j]))
        score = jnp.concatenate(scores, axis=0)
        prob = jnp.where(limits[k], jnp.exp(ATTN_CAP * jnp.tanh(score / ATTN_CAP)), 0.0)
        denom = jnp.sum(prob, axis=1, keepdims=True)
        for j in range(8):
            pj = prob[j * 8:(j + 1) * 8, :].astype(BF16)
            full = nn_dot(pj, values[j])
            mine = jnp.zeros((8, 128), F32)
            for b in range(4):
                mine = jnp.where(lane_head[0:8, :] == b, full[:, b * 128:(b + 1) * 128], mine)
            s3[k * 8 + j, 0:8, :] = mine
            s3[k * 8 + j, 8:9, :] = column_to_row(denom[j * 8:(j + 1) * 8, :])

    tile_guide = lax.rem(s, 2)
    holds_tile = g == tile_guide

    def send_tile(off, carry):
        i = lax.rem(s + off, NS)
        send(s3.at[i], r3.at[me], 2, {"guide": lax.rem(i, 2), "seq": i})
        return carry

    lax.fori_loop(1, NS, send_tile, 0)

    @pl.when(jnp.logical_not(holds_tile))
    def _():
        send(s3.at[s], r3.at[me], 2, {"guide": tile_guide, "seq": s})

    pending.append((s3.at[pl.ds(0, NS - 1)], 2, holds_tile))
    pending.append((s3, 2, jnp.logical_not(holds_tile)))
    pending.append((s1.at[pl.ds(0, NP - 1), pl.ds(0, 8)], 3, holds_tile))

    for k in range(NG):
        kx = nn_dot(picks[k][1], gathered[k])
        vx = nn_dot(picks[k][2], gathered[k])
        for j in range(8):
            ks[k * 8 + j] = kx[j * 8:(j + 1) * 8, :]
            vs[k * 8 + j] = vx[j * 8:(j + 1) * 8, :]

    ffw_combine(set_a, 6)
    loads[11].wait()
    pick_table(0, 1)

    @pl.when(holds_tile)
    def _():
        r3[me] = s3[s]
        own = jnp.exp(ATTN_CAP * jnp.tanh(jnp.sum(qs[s] * ks[s], axis=1, keepdims=True) / ATTN_CAP))
        whole(r3.at[pl.ds(0, NP - 1)], 2).wait_recv()
        sums = jnp.sum(r3[...], axis=0)
        numer = sums[0:8, :] + own.astype(BF16).astype(F32) * vs[s]
        den = row_to_column(sums[8:9, :], 8) + own
        b4[s] = (numer / den).astype(BF16).astype(F32)
        to_plane(lambda g2, s2: send(b4.at[s], b4.at[s], 3, {"guide": g2, "seq": s2}))

    r_ = iota((128, 128), 0)
    c_ = iota((128, 128), 1)
    held = jnp.zeros((128, 128), jnp.int32)
    for i in range(16):
        held = jnp.where(lax.div(c_, 8) == i, owner[i // 8, i % 8], held)
    back = one_hot(
        (lax.div(r_, 16) == lax.rem(c_, 8))
        & (lax.rem(lax.div(r_, 8), 2) == lax.div(c_, 64))
        & (lax.rem(r_, 8) == held)
    )
    pick_table(1, 2)
    loads[7].wait()

    @pl.when(holds_tile)
    def _():
        whole(b4.at[pl.ds(0, NS - 1)], 3).wait_recv()

    @pl.when(jnp.logical_not(holds_tile))
    def _():
        whole(b4, 3).wait_recv()

    att = nn_dot(back, b4[...].reshape(128, 128).astype(BF16))
    att = jnp.concatenate([att[h * 16:(h + 1) * 16, :] for h in range(8)], axis=1).astype(BF16)
    b5[kv] = nt_dot(att, w_o[...])
    to_kv(lambda k2: send(b5.at[kv], b5.at[kv], 4, {"kv": k2}))
    pending.append((b5.at[pl.ds(0, NKV - 1)], 4, None))
    ffw_send(set_a, 17)
    pick_table(3, 1)
    whole(b5.at[pl.ds(0, NKV - 1)], 4).wait_recv()
    projected = (b5[0] + b5[1]) + (b5[2] + b5[3])
    branch = projected * gain1[...]
    b6[me, 0:1, :] = column_to_row(jnp.sum(projected * projected, axis=-1, keepdims=True))
    b6[me, 1:2, :] = column_to_row(jnp.sum(x_in * branch, axis=-1, keepdims=True))
    b6[me, 2:3, :] = column_to_row(jnp.sum(branch * branch, axis=-1, keepdims=True))
    b6[me, 3:4, :] = x_sq
    to_plane(lambda g2, s2: send(b6.at[me], b6.at[me], 5, {"guide": g2, "seq": s2}))
    pending.append((b6.at[pl.ds(0, NP - 1)], 5, None))
    ffw_product(branch * gain2[...], set_b, 19)
    ffw_combine(set_b, 19)
    ffw_send(set_b, 21)
    pick_table(4, 3)
    whole(b6.at[pl.ds(0, NP - 1)], 5).wait_recv()
    sums = jnp.sum(b6[...], axis=0)
    out_scale = lax.rsqrt(row_to_column(sums[0:1, :], 16) / D + EPS)
    middle_sq = (
        row_to_column(sums[3:4, :], 16)
        + 2.0 * out_scale * row_to_column(sums[1:2, :], 16)
        + out_scale * out_scale * row_to_column(sums[2:3, :], 16)
    )
    ffw_scale = lax.rsqrt(jnp.maximum(middle_sq, 0.0) / D + EPS)
    bm[s, 0:16, :] = x_in + branch * out_scale
    bm[s, 16:17, :] = gain3[...]
    bm[s, 17:18, :] = gain4[...]

    def activate(first, second):
        n = first.shape[1] // 2
        both = (first + out_scale * second) * ffw_scale
        return (jax.nn.gelu(both[:, 0:n], approximate=True) * both[:, n:2 * n]).astype(BF16)

    def gathered_sum(ref):
        return jnp.sum(ref[...].astype(F32), axis=0)

    whole(ra.at[pl.ds(0, NS - 1)], 17).wait_recv()
    first = gathered_sum(ra)
    whole(rb.at[pl.ds(0, NS - 1)], 21).wait_recv()
    mine = pl.ds(pl.multiple_of(me * FB, FB), FB)
    act[:, mine] = activate(first, gathered_sum(rb))
    to_plane(lambda g2, s2: send(act.at[:, mine], act.at[:, mine], 10, {"guide": g2, "seq": s2}))
    pending.append((act.at[:, pl.ds(0, (NP - 1) * FB)], 10, None))
    pending.append((act.at[:, pl.ds(0, (NP - 1) * 128)], 11, holds_extra))

    @pl.when(holds_extra)
    def _():
        own = extra - 4 * g
        xa[s] = wa[own]
        xb[s] = wb[own]
        whole(xa.at[pl.ds(0, NS - 1)], 18).wait_recv()
        whole(xb.at[pl.ds(0, NS - 1)], 22).wait_recv()
        cols = pl.ds(pl.multiple_of(tail + extra * 128, 128), 128)
        act[:, cols] = activate(gathered_sum(xa), gathered_sum(xb))
        to_plane(lambda g2, s2: send(act.at[:, cols], act.at[:, cols], 11, {"guide": g2, "seq": s2}))

    pick_table(7, 2)
    loads[10].wait()
    whole(act.at[:, pl.ds(0, (NP - 1) * FB)], 10).wait_recv()

    @pl.when(holds_extra)
    def _():
        whole(act.at[:, pl.ds(0, (EXTRA - 1) * 128)], 11).wait_recv()

    @pl.when(jnp.logical_not(holds_extra))
    def _():
        whole(act.at[:, pl.ds(0, EXTRA * 128)], 11).wait_recv()

    to_plane(lambda g2, s2: send(bm.at[s], bm.at[s], 9, {"seq": s2}), NS)
    pending.append((bm.at[pl.ds(0, NS - 1)], 9, None))
    b12[kv] = nt_dot(act[...], w_d[...])
    to_kv(lambda k2: send(b12.at[kv], b12.at[kv], 12, {"kv": k2}))
    pending.append((b12.at[pl.ds(0, NKV - 1)], 12, None))
    whole(b12.at[pl.ds(0, NKV - 1)], 12).wait_recv()
    ffw_out = (b12[0] + b12[1]) + (b12[2] + b12[3])
    b14[s] = ffw_out.astype(BF16)
    b13[me] = column_to_row(jnp.sum(ffw_out * ffw_out, axis=-1, keepdims=True))
    to_plane(lambda g2, s2: send(b14.at[s], b14.at[s], 14, {"seq": s2}), NS)
    pending.append((b14.at[pl.ds(0, NS - 1)], 14, None))
    to_plane(lambda g2, s2: send(b13.at[me], b13.at[me], 13, {"guide": g2, "seq": s2}))
    pending.append((b13.at[pl.ds(0, NP - 1)], 13, None))

    whole(bm.at[pl.ds(0, NS - 1)], 9).wait_recv()
    whole(b13.at[pl.ds(0, NP - 1)], 13).wait_recv()
    branch_scale = lax.rsqrt(row_to_column(jnp.sum(b13[...], axis=0), 16) / D + EPS)
    whole(b14.at[pl.ds(0, NS - 1)], 14).wait_recv()
    last_sq = jnp.zeros((16, 1), F32)
    for t in range(NS):
        last = bm[t, 0:16, :] + b14[t].astype(F32) * branch_scale * bm[t, 16:17, :]
        last_sq = last_sq + jnp.sum(last * last, axis=-1, keepdims=True)
        rows_f[:, t * WL:(t + 1) * WL] = last * bm[t, 17:18, :]
    s15[...] = column_to_row(last_sq)
    send(s15, r15, 15, other)
    pending.append((s15, 15, None))

    logit = nn_dot(rows_f[...].astype(BF16), table[...])
    lower = jnp.concatenate([logit[0:4, :], logit[8:12, :]], axis=0)
    upper = jnp.concatenate([logit[4:8, :], logit[12:16, :]], axis=0)
    s16[...] = jnp.where(g == 0, upper, lower)
    send(s16, r16, 16, other)
    pending.append((s16, 16, None))
    keep = jnp.where(g == 0, lower, upper)
    whole(r15, 15).wait_recv()
    lanes = iota((8, 128), 1)
    rowi = iota((8, 128), 0)
    want = lax.div(rowi, 4) * 8 + 4 * g + lax.rem(rowi, 4)
    sq = jnp.sum(jnp.where(lanes == want, jnp.broadcast_to(s15[...] + r15[...], (8, 128)), 0.0),
                 axis=1, keepdims=True)
    final_scale = lax.rsqrt(sq / D + EPS)
    share = jnp.zeros((4, 1), F32)
    for i in range(4):
        share = jnp.where(iota((4, 1), 0) == i, guidance[4 * g + i], share)
    whole(r16, 16).wait_recv()
    capped = LOGIT_CAP * jnp.tanh((keep + r16[...]) * final_scale / LOGIT_CAP)
    base_ref[...] = capped[4:8, :]
    lift_ref[...] = share * (capped[0:4, :] - capped[4:8, :])

    finish()


def on_device(
    hidden, lengths, slot_owner, allowed_ids, guidance,
    pre_attn_gain, post_attn_gain, pre_ffw_gain, post_ffw_gain, final_gain,
    query_weight, key_weight, value_weight, output_weight,
    gate_weight, up_weight, down_weight, embedding,
    cond_keys, cond_values, uncond_keys, uncond_values,
):
    lane = np.arange(HD) % (HD // 2)
    freq = jnp.asarray((THETA ** (-2.0 * lane / HD)).astype(np.float32).reshape(1, HD))
    gains = [
        gain.reshape(1, WL)
        for gain in (pre_attn_gain, post_attn_gain, pre_ffw_gain, post_ffw_gain, final_gain)
    ]
    smem = pl.BlockSpec(memory_space=pltpu.SMEM)
    vmem = pl.BlockSpec(memory_space=pltpu.VMEM)
    hbm = pl.BlockSpec(memory_space=pl.ANY)
    base, lift = pl.pallas_call(
        step_kernel,
        out_shape=[jax.ShapeDtypeStruct((4, PICK), F32)] * 2,
        in_specs=[smem] * 3 + [vmem] * 8 + [hbm] * 12,
        out_specs=[vmem] * 2,
        scratch_shapes=[
            pltpu.VMEM((WL, 2048), BF16),
            pltpu.VMEM((WL, 1024), BF16),
            pltpu.VMEM((WL, FFL), BF16),
            pltpu.VMEM((WL, FFL), BF16),
            pltpu.VMEM((WL, FFL), BF16),
            pltpu.VMEM((ROWS, HALF), BF16),
            pltpu.VMEM((8, 256, 512), BF16),
            pltpu.VMEM((8, 256, 512), BF16),
            pltpu.VMEM((8, 64, 512), BF16),
            pltpu.VMEM((8, 64, 512), BF16),
            pltpu.VMEM((ROWS, PICK), BF16),
            pltpu.VMEM((HALF, PICK), BF16),
            pltpu.VMEM((16, 8, 128), F32),
            pltpu.VMEM((16, 8, 128), F32),
            pltpu.VMEM((16, 8, 128), F32),
            pltpu.VMEM((16, HALF), F32),
            pltpu.VMEM((NP, 9, 128), F32),
            pltpu.VMEM((NP, 9, 128), F32),
            pltpu.VMEM((NP, 8, 128), F32),
            pltpu.VMEM((16, 9, 128), F32),
            pltpu.VMEM((NP, 9, 128), F32),
            pltpu.VMEM((16, 8, 128), F32),
            pltpu.VMEM((NKV, 16, WL), F32),
            pltpu.VMEM((NP, 4, 128), F32),
            pltpu.VMEM((NS, 18, WL), F32),
            pltpu.VMEM((16, FFL), BF16),
            pltpu.VMEM((NKV, 16, WL), F32),
            pltpu.VMEM((NP, 1, 128), F32),
            pltpu.VMEM((NS, 16, WL), BF16),
            pltpu.VMEM((8, PICK), F32),
            pltpu.VMEM((8, PICK), F32),
            pltpu.VMEM((1, 128), F32),
            pltpu.VMEM((1, 128), F32),
            *[
                pltpu.VMEM(shape, kind)
                for _ in range(2)
                for shape, kind in (
                    ((NS, 16, 2 * FB), BF16),
                    ((NS, 16, 2 * FB), BF16),
                    ((NS, 16, 2 * FB), F32),
                    ((NS, 16, 2 * FB), BF16),
                    ((NS, 16, 2 * FB), BF16),
                    ((4, 16, FB), BF16),
                    ((4, 16, FB), BF16),
                    ((4, 16, FB), F32),
                    ((4, 16, FB), BF16),
                    ((NS, 16, FB), BF16),
                )
            ],
            pltpu.SemaphoreType.DMA((12,)),
            pltpu.SemaphoreType.DMA((24,)),
            pltpu.SemaphoreType.DMA((24,)),
        ],
        compiler_params=pltpu.CompilerParams(
            collective_id=0, has_side_effects=True, vmem_limit_bytes=60 * 1024 * 1024
        ),
        name="decode_step",
    )(
        lengths, slot_owner, guidance, hidden, allowed_ids.reshape(8, 128), freq, *gains,
        query_weight, key_weight, value_weight, output_weight.T, gate_weight, up_weight, down_weight.T,
        embedding, cond_keys, cond_values, uncond_keys, uncond_values,
    )
    return base + lift


def solution(mesh):
    return jax.shard_map(
        on_device,
        mesh=mesh,
        in_specs=(
            P(None, None, ("guide", "seq")),
            P(),
            P(),
            P(("kv", "seq")),
            P(),
            P(("guide", "seq")),
            P(("guide", "seq")),
            P(("guide", "seq")),
            P(("guide", "seq")),
            P(("guide", "seq")),
            P(("guide", "seq"), "kv"),
            P(("guide", "seq"), "kv"),
            P(("guide", "seq"), "kv"),
            P("kv", ("guide", "seq")),
            P(("guide", "seq"), "kv"),
            P(("guide", "seq"), "kv"),
            P("kv", ("guide", "seq")),
            P(("kv", "seq"), "guide"),
            P(None, ("guide", "seq"), "kv"),
            P(None, ("guide", "seq"), "kv"),
            P(None, ("guide", "seq"), "kv"),
            P(None, ("guide", "seq"), "kv"),
        ),
        out_specs=P("guide", ("kv", "seq")),
        check_vma=False,
    )
```

```python
import functools

import jax
import jax.numpy as jnp
import numpy as np
from jax import lax
from jax.experimental import pallas as pl
from jax.experimental.pallas import tpu as pltpu
from jax.sharding import PartitionSpec as P

D = 4608
H = 32
HD = 128
EPS = 1e-06
ATTN_CAP = 50.0
LOGIT_CAP = 30.0
THETA = 10000.0
MESH = pl.DeviceIdType.MESH
F32 = jnp.float32
BF16 = jnp.bfloat16
NG, NKV, NS = 2, 4, 16
NP = NG * NS
WL = D // NP
FFL = 9216
FB = 256
EXTRA = 8
ROWS = 2048
HALF = D // 2
PICK = 1024


def iota(shape, dim):
    return lax.broadcasted_iota(jnp.int32, shape, dim)


def column_to_row(col):
    n = col.shape[0]
    spread = jnp.where(iota((n, 128), 0) == iota((n, 128), 1), jnp.broadcast_to(col, (n, 128)), 0.0)
    return jnp.sum(spread, axis=0, keepdims=True)


def row_to_column(row, n, first=0):
    lanes = iota((n, 128), 1)
    picked = jnp.where(lanes == iota((n, 128), 0) + first, jnp.broadcast_to(row, (n, 128)), 0.0)
    return jnp.sum(picked, axis=1, keepdims=True)


def nt_dot(a, b):
    return lax.dot_general(a, b, (((1,), (1,)), ((), ())), preferred_element_type=F32)


def nn_dot(a, b):
    return jnp.dot(a, b, preferred_element_type=F32)


def one_hot(mask):
    return jnp.where(mask, 1.0, 0.0).astype(BF16)


def step_kernel(
    lengths_h, owner_h, guidance_h, hidden_h, ids_h, freq_h, gain0_h, gain1_h, gain2_h, gain3_h, gain4_h,
    qw_h, kw_h, vw_h, ow_h, gw_h, uw_h, dw_h, emb_h, ck_h, cv_h, uk_h, uv_h,
    base_ref, lift_ref,
    w_qkv, w_o, w_g, w_u, w_d, emb, ck, cv, uk, uv,
    pick, table, qs, ks, vs, rows_f,
    s1, r1, b2, s3, r3, b4, b5, b6, bm, act, b12, b13, b14, s16, r16,
    pa, qa, ka, sa, ra, ta, ua, va, wa, xa, pb, qb, kb, sb, rb, tb, ub, vb, wb, xb,
    lengths, owner, guidance, hidden, ids, freq, gain0, gain1, gain2, gain3, gain4,
    load_sem, send_sem, recv_sem,
):
    g = lax.axis_index("guide")
    kv = lax.axis_index("kv")
    s = lax.axis_index("seq")
    z = lax.div(s, 4)
    x = lax.rem(s, 4)
    me = g * NS + s

    loads = [
        pltpu.make_async_copy(src, dst, load_sem.at[i])
        for i, (src, dst) in enumerate(
            [
                (qw_h, w_qkv.at[:, pl.ds(0, 1024)]),
                (kw_h, w_qkv.at[:, pl.ds(1024, 512)]),
                (vw_h, w_qkv.at[:, pl.ds(1536, 512)]),
                (ck_h, ck),
                (uk_h, uk),
                (cv_h, cv),
                (uv_h, uv),
                (ow_h, w_o),
                (gw_h, w_g),
                (uw_h, w_u),
                (dw_h, w_d),
                (emb_h, emb),
                (hidden_h, hidden),
                (gain0_h, gain0),
                (lengths_h, lengths),
                (owner_h, owner),
                (guidance_h, guidance),
                (ids_h, ids),
                (freq_h, freq),
                (gain1_h, gain1),
                (gain2_h, gain2),
                (gain3_h, gain3),
                (gain4_h, gain4),
            ]
        )
    ]

    def peer(off):
        g2 = lax.rem(g + lax.div(off, 16), 2)
        z2 = lax.rem(z + lax.div(lax.rem(off, 16), 4), 4)
        x2 = lax.rem(x + lax.rem(off, 4), 4)
        return g2, z2 * 4 + x2

    def to_plane(body, count=NP):
        def one(off, carry):
            g2, s2 = peer(off)
            body(g2, s2)
            return carry

        lax.fori_loop(1, count, one, 0)

    def to_kv(body):
        for off in range(1, NKV):
            body(lax.rem(kv + off, NKV))

    def send(src, dst, i, device):
        pltpu.make_async_remote_copy(
            src_ref=src, dst_ref=dst, send_sem=send_sem.at[i], recv_sem=recv_sem.at[i],
            device_id=device, device_id_type=MESH,
        ).start()

    def whole(ref, i):
        return pltpu.make_async_remote_copy(
            src_ref=ref, dst_ref=ref, send_sem=send_sem.at[i], recv_sem=recv_sem.at[i],
            device_id={"guide": lax.rem(g + 1, 2)}, device_id_type=MESH,
        )

    pending = []

    def finish():
        for ref, i, when in pending:
            if when is None:
                whole(ref, i).wait_send()
            else:
                pl.when(when)(functools.partial(lambda ref, i: whole(ref, i).wait_send(), ref, i))

    barrier = pltpu.get_barrier_semaphore()
    to_plane(lambda g2, s2: pl.semaphore_signal(
        barrier, inc=1, device_id={"guide": g2, "seq": s2}, device_id_type=MESH))
    to_kv(lambda k2: pl.semaphore_signal(barrier, inc=1, device_id={"kv": k2}, device_id_type=MESH))

    for load in loads[12:23] + loads[0:3]:
        load.start()
    other = {"guide": lax.rem(g + 1, 2)}
    tail = NP * FB
    holds_extra = (lax.rem(x, 2) == lax.rem(z, 2)) & (lax.div(z, 2) == g)
    extra = 2 * z + lax.div(x, 2)
    set_a = (pa, qa, ka, sa, ra, ta, ua, va, wa, xa)
    set_b = (pb, qb, kb, sb, rb, tb, ub, vb, wb, xb)

    def ffw_product(rows, buffers, base):
        away, _, keep, _, _, tail_away, _, tail_keep, _, _ = buffers
        high = rows.astype(BF16)
        low = (rows - high.astype(F32)).astype(BF16)
        both = jnp.concatenate([high, low], axis=0)

        def product(weight, cols):
            wide = nn_dot(both, weight[:, cols])
            return wide[0:16, :] + wide[16:32, :]

        for whose, main, rest in ((1 - g, away, tail_away), (g, keep, tail_keep)):
            cols = pl.ds(pl.multiple_of(whose * (NS * FB), NS * FB), NS * FB)
            tail_cols = pl.ds(pl.multiple_of(tail + whose * 512, 512), 512)
            for at, weight in ((0, w_g), (1, w_u)):
                part = product(weight, cols).astype(main.dtype)
                for c in range(NS):
                    main[c, :, at * FB:(at + 1) * FB] = part[:, c * FB:(c + 1) * FB]
                part = product(weight, tail_cols).astype(rest.dtype)
                for c in range(4):
                    rest[c, :, at * 128:(at + 1) * 128] = part[:, c * 128:(c + 1) * 128]
            if main is away:
                send(away, buffers[1], base, other)
                send(tail_away, buffers[6], base + 1, other)
                pending.append((away, base, None))
                pending.append((tail_away, base + 1, None))

    def ffw_combine(buffers, base):
        _, came, keep, out, _, _, tail_came, tail_keep, tail_out, _ = buffers
        whole(came, base).wait_recv()
        whole(tail_came, base + 1).wait_recv()
        out[...] = (keep[...] + came[...].astype(F32)).astype(BF16)
        tail_out[...] = (tail_keep[...] + tail_came[...].astype(F32)).astype(BF16)

    def ffw_send(buffers, base):
        _, _, _, out, into, _, _, _, tail_out, tail_into = buffers

        def one(q, carry):
            z2 = 2 * g + lax.div(q, 2)
            s2 = 4 * z2 + 2 * lax.rem(q, 2) + lax.rem(z2, 2)

            @pl.when(s2 != s)
            def _():
                send(tail_out.at[q], tail_into.at[s], base + 1, {"seq": s2})

            return carry

        lax.fori_loop(0, 4, one, 0)
        to_plane(lambda g2, s2: send(out.at[s2], into.at[s], base, {"seq": s2}), NS)
        into[s] = out[s]
        pending.append((out.at[pl.ds(0, NS - 1)], base, None))
        pending.append((tail_out.at[pl.ds(0, 3)], base + 1, holds_extra))
        pending.append((tail_out, base + 1, jnp.logical_not(holds_extra)))

    for load in loads[12:23]:
        load.wait()
    x_in = hidden[...].astype(F32).reshape(16, WL)
    normed = (x_in * gain0[...]).astype(BF16)
    x_sq = column_to_row(jnp.sum(x_in * x_in, axis=-1, keepdims=True))
    for i in range(3):
        loads[i].wait()
    for load in loads[3:12]:
        load.start()
    part = nn_dot(normed, w_qkv[...])
    for j in range(NS):
        for k in range(NG):
            s1[k * NS + j, 0:8, :] = part[k * 8:(k + 1) * 8, j * 128:(j + 1) * 128]
            s1[k * NS + j, 8:9, :] = x_sq
    r1[me] = s1[me]

    first_row = (kv * NS + s) * ROWS

    def pick_rows(i, carry):
        base = pl.multiple_of(i * 256, 256)
        v = iota((256, 128), 0) + (first_row + base)
        for c in range(PICK // 128):
            pick[pl.ds(base, 256), c * 128:(c + 1) * 128] = one_hot(v == ids[c:c + 1, :])
        return carry

    def pick_table(first, count):
        def one(i, carry):
            cols = pl.ds(pl.multiple_of(i * 256, 256), 256)
            table[cols, :] = lax.dot_general(
                emb[:, cols], pick[...], (((0,), (0,)), ((), ())), preferred_element_type=F32
            ).astype(BF16)
            return carry

        lax.fori_loop(first, first + count, one, 0)

    turn_row = iota((8, 128), 0)
    position = jnp.zeros((8, 128), F32)
    for i in range(8):
        position = jnp.where(turn_row == i, lengths[g, i].astype(F32), position)
    angle = position * freq[...]
    cosine = jnp.cos(angle)
    sine = jnp.sin(angle)
    sine = jnp.where(iota((8, 128), 1) < 64, -sine, sine)
    pl.semaphore_wait(barrier, NP - 1 + NKV - 1)
    to_plane(lambda g2, s2: send(
        s1.at[g2 * NS + s2], r1.at[me], 0, {"guide": g2, "seq": s2}))
    pending.append((s1.at[pl.ds(0, NP - 1)], 0, None))

    lax.fori_loop(0, ROWS // 256, pick_rows, 0)
    whole(r1.at[pl.ds(0, NP - 1)], 0).wait_recv()
    total = jnp.sum(r1[...], axis=0)
    scale = lax.rsqrt(row_to_column(total[8:9, :], 8, 8 * g) / D + EPS)
    y = total[0:8, :] * scale
    turned = y * cosine + pltpu.roll(y, 64, 1) * sine
    y = jnp.where(s < 12, turned, y)
    y = jnp.where(s < 8, y * (D // H) ** (-0.5), y)
    b2[me] = y.astype(BF16).astype(F32)
    to_plane(lambda g2, s2: send(b2.at[me], b2.at[me], 1, {"guide": g2, "seq": s2}))
    pending.append((b2.at[pl.ds(0, NP - 1)], 1, None))

    picks = []
    r_ = iota((64, 128), 0)
    c_ = iota((64, 128), 1)
    for k in range(NG):
        held = jnp.zeros((64, 128), jnp.int32)
        for j in range(8):
            held = jnp.where(lax.div(r_, 8) == j, owner[k, j], held)
        same = lax.rem(c_, 8) == held
        head = lax.rem(r_, 8)
        blk = lax.div(c_, 8)
        picks.append((
            one_hot(same & (blk == head)),
            one_hot(same & (blk == 8 + lax.div(head, 2))),
            one_hot(same & (blk == 12 + lax.div(head, 2))),
        ))
    block = me
    limits = []
    for k, span in ((0, 256), (1, 64)):
        limit = jnp.zeros((64, span), jnp.int32)
        row = lax.div(iota((64, span), 0), 8)
        for j in range(8):
            limit = jnp.where(row == j, lengths[k, owner[k, j]], limit)
        limits.append(iota((64, span), 1) + block * span < limit)

    loads[8].wait()
    loads[9].wait()
    ffw_product(x_in * gain2[...], set_a, 6)
    for i in range(3, 7):
        loads[i].wait()
    whole(b2.at[pl.ds(0, NP - 1)], 1).wait_recv()
    gathered = b2[...].reshape(NG, 128, 128).astype(BF16)
    lane_head = lax.div(lax.rem(iota((64, 128), 0), 8), 2)
    for k, span, keys, values in ((0, 256, ck, cv), (1, 64, uk, uv)):
        q = nn_dot(picks[k][0], gathered[k])
        for j in range(8):
            qs[k * 8 + j] = q[j * 8:(j + 1) * 8, :]
        wide = [jnp.where(lane_head == b, q, 0.0) for b in range(4)]
        scores = []
        for j in range(8):
            qj = jnp.concatenate([w[j * 8:(j + 1) * 8, :] for w in wide], axis=1).astype(BF16)
            scores.append(nt_dot(qj, keys[j]))
        score = jnp.concatenate(scores, axis=0)
        prob = jnp.where(limits[k], jnp.exp(ATTN_CAP * jnp.tanh(score / ATTN_CAP)), 0.0)
        denom = jnp.sum(prob, axis=1, keepdims=True)
        for j in range(8):
            pj = prob[j * 8:(j + 1) * 8, :].astype(BF16)
            full = nn_dot(pj, values[j])
            mine = jnp.zeros((8, 128), F32)
            for b in range(4):
                mine = jnp.where(lane_head[0:8, :] == b, full[:, b * 128:(b + 1) * 128], mine)
            s3[k * 8 + j, 0:8, :] = mine
            s3[k * 8 + j, 8:9, :] = column_to_row(denom[j * 8:(j + 1) * 8, :])

    tile_guide = lax.rem(s, 2)
    holds_tile = g == tile_guide

    def send_tile(off, carry):
        i = lax.rem(s + off, NS)
        send(s3.at[i], r3.at[me], 2, {"guide": lax.rem(i, 2), "seq": i})
        return carry

    lax.fori_loop(1, NS, send_tile, 0)

    @pl.when(jnp.logical_not(holds_tile))
    def _():
        send(s3.at[s], r3.at[me], 2, {"guide": tile_guide, "seq": s})

    pending.append((s3.at[pl.ds(0, NS - 1)], 2, holds_tile))
    pending.append((s3, 2, jnp.logical_not(holds_tile)))
    pending.append((s1.at[pl.ds(0, NP - 1), pl.ds(0, 8)], 3, holds_tile))

    for k in range(NG):
        kx = nn_dot(picks[k][1], gathered[k])
        vx = nn_dot(picks[k][2], gathered[k])
        for j in range(8):
            ks[k * 8 + j] = kx[j * 8:(j + 1) * 8, :]
            vs[k * 8 + j] = vx[j * 8:(j + 1) * 8, :]

    ffw_combine(set_a, 6)
    loads[11].wait()
    pick_table(0, 1)

    @pl.when(holds_tile)
    def _():
        r3[me] = s3[s]
        own = jnp.exp(ATTN_CAP * jnp.tanh(jnp.sum(qs[s] * ks[s], axis=1, keepdims=True) / ATTN_CAP))
        whole(r3.at[pl.ds(0, NP - 1)], 2).wait_recv()
        sums = jnp.sum(r3[...], axis=0)
        numer = sums[0:8, :] + own.astype(BF16).astype(F32) * vs[s]
        den = row_to_column(sums[8:9, :], 8) + own
        b4[s] = (numer / den).astype(BF16).astype(F32)
        to_plane(lambda g2, s2: send(b4.at[s], b4.at[s], 3, {"guide": g2, "seq": s2}))

    r_ = iota((128, 128), 0)
    c_ = iota((128, 128), 1)
    held = jnp.zeros((128, 128), jnp.int32)
    for i in range(16):
        held = jnp.where(lax.div(c_, 8) == i, owner[i // 8, i % 8], held)
    back = one_hot(
        (lax.div(r_, 16) == lax.rem(c_, 8))
        & (lax.rem(lax.div(r_, 8), 2) == lax.div(c_, 64))
        & (lax.rem(r_, 8) == held)
    )
    pick_table(1, 2)
    loads[7].wait()

    @pl.when(holds_tile)
    def _():
        whole(b4.at[pl.ds(0, NS - 1)], 3).wait_recv()

    @pl.when(jnp.logical_not(holds_tile))
    def _():
        whole(b4, 3).wait_recv()

    att = nn_dot(back, b4[...].reshape(128, 128).astype(BF16))
    att = jnp.concatenate([att[h * 16:(h + 1) * 16, :] for h in range(8)], axis=1).astype(BF16)
    b5[kv] = nt_dot(att, w_o[...])
    to_kv(lambda k2: send(b5.at[kv], b5.at[kv], 4, {"kv": k2}))
    pending.append((b5.at[pl.ds(0, NKV - 1)], 4, None))
    ffw_send(set_a, 17)
    pick_table(3, 1)
    whole(b5.at[pl.ds(0, NKV - 1)], 4).wait_recv()
    projected = (b5[0] + b5[1]) + (b5[2] + b5[3])
    branch = projected * gain1[...]
    ffw_product(branch * gain2[...], set_b, 19)
    b6[me, 0:1, :] = column_to_row(jnp.sum(projected * projected, axis=-1, keepdims=True))
    b6[me, 1:2, :] = column_to_row(jnp.sum(x_in * branch, axis=-1, keepdims=True))
    b6[me, 2:3, :] = column_to_row(jnp.sum(branch * branch, axis=-1, keepdims=True))
    b6[me, 3:4, :] = x_sq
    to_plane(lambda g2, s2: send(b6.at[me], b6.at[me], 5, {"guide": g2, "seq": s2}))
    pending.append((b6.at[pl.ds(0, NP - 1)], 5, None))
    ffw_combine(set_b, 19)
    ffw_send(set_b, 21)
    pick_table(4, 3)
    whole(b6.at[pl.ds(0, NP - 1)], 5).wait_recv()
    sums = jnp.sum(b6[...], axis=0)
    out_scale = lax.rsqrt(row_to_column(sums[0:1, :], 16) / D + EPS)
    middle_sq = (
        row_to_column(sums[3:4, :], 16)
        + 2.0 * out_scale * row_to_column(sums[1:2, :], 16)
        + out_scale * out_scale * row_to_column(sums[2:3, :], 16)
    )
    ffw_scale = lax.rsqrt(jnp.maximum(middle_sq, 0.0) / D + EPS)
    bm[s, 0:16, :] = x_in + branch * out_scale
    bm[s, 16:17, :] = gain3[...]
    bm[s, 17:18, :] = gain4[...]

    def activate(first, second):
        n = first.shape[1] // 2
        both = (first + out_scale * second) * ffw_scale
        return (jax.nn.gelu(both[:, 0:n], approximate=True) * both[:, n:2 * n]).astype(BF16)

    def gathered_sum(ref):
        return jnp.sum(ref[...].astype(F32), axis=0)

    whole(ra.at[pl.ds(0, NS - 1)], 17).wait_recv()
    first = gathered_sum(ra)
    whole(rb.at[pl.ds(0, NS - 1)], 21).wait_recv()
    mine = pl.ds(pl.multiple_of(me * FB, FB), FB)
    act[:, mine] = activate(first, gathered_sum(rb))
    to_plane(lambda g2, s2: send(act.at[:, mine], act.at[:, mine], 10, {"guide": g2, "seq": s2}))
    pending.append((act.at[:, pl.ds(0, (NP - 1) * FB)], 10, None))
    pending.append((act.at[:, pl.ds(0, (NP - 1) * 128)], 11, holds_extra))

    @pl.when(holds_extra)
    def _():
        own = extra - 4 * g
        xa[s] = wa[own]
        xb[s] = wb[own]
        whole(xa.at[pl.ds(0, NS - 1)], 18).wait_recv()
        whole(xb.at[pl.ds(0, NS - 1)], 22).wait_recv()
        cols = pl.ds(pl.multiple_of(tail + extra * 128, 128), 128)
        act[:, cols] = activate(gathered_sum(xa), gathered_sum(xb))
        to_plane(lambda g2, s2: send(act.at[:, cols], act.at[:, cols], 11, {"guide": g2, "seq": s2}))

    pick_table(7, 2)
    loads[10].wait()
    whole(act.at[:, pl.ds(0, (NP - 1) * FB)], 10).wait_recv()

    @pl.when(holds_extra)
    def _():
        whole(act.at[:, pl.ds(0, (EXTRA - 1) * 128)], 11).wait_recv()

    @pl.when(jnp.logical_not(holds_extra))
    def _():
        whole(act.at[:, pl.ds(0, EXTRA * 128)], 11).wait_recv()

    to_plane(lambda g2, s2: send(bm.at[s], bm.at[s], 9, {"seq": s2}), NS)
    pending.append((bm.at[pl.ds(0, NS - 1)], 9, None))
    b12[kv] = nt_dot(act[...], w_d[...])
    to_kv(lambda k2: send(b12.at[kv], b12.at[kv], 12, {"kv": k2}))
    pending.append((b12.at[pl.ds(0, NKV - 1)], 12, None))
    whole(b12.at[pl.ds(0, NKV - 1)], 12).wait_recv()
    ffw_out = (b12[0] + b12[1]) + (b12[2] + b12[3])
    b14[s] = ffw_out.astype(BF16)
    b13[me] = column_to_row(jnp.sum(ffw_out * ffw_out, axis=-1, keepdims=True))
    to_plane(lambda g2, s2: send(b14.at[s], b14.at[s], 14, {"seq": s2}), NS)
    pending.append((b14.at[pl.ds(0, NS - 1)], 14, None))
    to_plane(lambda g2, s2: send(b13.at[me], b13.at[me], 13, {"guide": g2, "seq": s2}))
    pending.append((b13.at[pl.ds(0, NP - 1)], 13, None))

    whole(bm.at[pl.ds(0, NS - 1)], 9).wait_recv()
    whole(b13.at[pl.ds(0, NP - 1)], 13).wait_recv()
    branch_scale = lax.rsqrt(row_to_column(jnp.sum(b13[...], axis=0), 16) / D + EPS)
    whole(b14.at[pl.ds(0, NS - 1)], 14).wait_recv()
    last_sq = jnp.zeros((16, WL), F32)
    for t in range(NS):
        last = bm[t, 0:16, :] + b14[t].astype(F32) * branch_scale * bm[t, 16:17, :]
        last_sq = last_sq + last * last
        rows_f[:, t * WL:(t + 1) * WL] = last * bm[t, 17:18, :]
    sq_row = column_to_row(jnp.sum(last_sq, axis=-1, keepdims=True))

    logit = nn_dot(rows_f[...].astype(BF16), table[...])
    lower = jnp.concatenate([logit[0:4, :], logit[8:12, :]], axis=0)
    upper = jnp.concatenate([logit[4:8, :], logit[12:16, :]], axis=0)
    s16[0:8, :] = jnp.where(g == 0, upper, lower)
    s16[8:9, 0:128] = sq_row
    send(s16, r16, 16, other)
    pending.append((s16, 16, None))
    keep = jnp.where(g == 0, lower, upper)
    whole(r16, 16).wait_recv()
    lanes = iota((8, 128), 1)
    rowi = iota((8, 128), 0)
    want = lax.div(rowi, 4) * 8 + 4 * g + lax.rem(rowi, 4)
    sq = jnp.sum(jnp.where(lanes == want, jnp.broadcast_to(sq_row + r16[8:9, 0:128], (8, 128)), 0.0),
                 axis=1, keepdims=True)
    final_scale = lax.rsqrt(sq / D + EPS)
    share = jnp.zeros((4, 1), F32)
    for i in range(4):
        share = jnp.where(iota((4, 1), 0) == i, guidance[4 * g + i], share)
    capped = LOGIT_CAP * jnp.tanh((keep + r16[0:8, :]) * final_scale / LOGIT_CAP)
    base_ref[...] = capped[4:8, :]
    lift_ref[...] = share * (capped[0:4, :] - capped[4:8, :])

    finish()


def on_device(
    hidden, lengths, slot_owner, allowed_ids, guidance,
    pre_attn_gain, post_attn_gain, pre_ffw_gain, post_ffw_gain, final_gain,
    query_weight, key_weight, value_weight, output_weight,
    gate_weight, up_weight, down_weight, embedding,
    cond_keys, cond_values, uncond_keys, uncond_values,
):
    lane = np.arange(HD) % (HD // 2)
    freq = jnp.asarray((THETA ** (-2.0 * lane / HD)).astype(np.float32).reshape(1, HD))
    gains = [
        gain.reshape(1, WL)
        for gain in (pre_attn_gain, post_attn_gain, pre_ffw_gain, post_ffw_gain, final_gain)
    ]
    vmem = pl.BlockSpec(memory_space=pltpu.VMEM)
    hbm = pl.BlockSpec(memory_space=pl.ANY)
    base, lift = pl.pallas_call(
        step_kernel,
        out_shape=[jax.ShapeDtypeStruct((4, PICK), F32)] * 2,
        in_specs=[hbm] * 23,
        out_specs=[vmem] * 2,
        scratch_shapes=[
            pltpu.VMEM((WL, 2048), BF16),
            pltpu.VMEM((WL, 1024), BF16),
            pltpu.VMEM((WL, FFL), BF16),
            pltpu.VMEM((WL, FFL), BF16),
            pltpu.VMEM((WL, FFL), BF16),
            pltpu.VMEM((ROWS, HALF), BF16),
            pltpu.VMEM((8, 256, 512), BF16),
            pltpu.VMEM((8, 256, 512), BF16),
            pltpu.VMEM((8, 64, 512), BF16),
            pltpu.VMEM((8, 64, 512), BF16),
            pltpu.VMEM((ROWS, PICK), BF16),
            pltpu.VMEM((HALF, PICK), BF16),
            pltpu.VMEM((16, 8, 128), F32),
            pltpu.VMEM((16, 8, 128), F32),
            pltpu.VMEM((16, 8, 128), F32),
            pltpu.VMEM((16, HALF), F32),
            pltpu.VMEM((NP, 9, 128), F32),
            pltpu.VMEM((NP, 9, 128), F32),
            pltpu.VMEM((NP, 8, 128), F32),
            pltpu.VMEM((16, 9, 128), F32),
            pltpu.VMEM((NP, 9, 128), F32),
            pltpu.VMEM((16, 8, 128), F32),
            pltpu.VMEM((NKV, 16, WL), F32),
            pltpu.VMEM((NP, 4, 128), F32),
            pltpu.VMEM((NS, 18, WL), F32),
            pltpu.VMEM((16, FFL), BF16),
            pltpu.VMEM((NKV, 16, WL), F32),
            pltpu.VMEM((NP, 1, 128), F32),
            pltpu.VMEM((NS, 16, WL), BF16),
            pltpu.VMEM((9, PICK), F32),
            pltpu.VMEM((9, PICK), F32),
            *[
                pltpu.VMEM(shape, kind)
                for _ in range(2)
                for shape, kind in (
                    ((NS, 16, 2 * FB), BF16),
                    ((NS, 16, 2 * FB), BF16),
                    ((NS, 16, 2 * FB), F32),
                    ((NS, 16, 2 * FB), BF16),
                    ((NS, 16, 2 * FB), BF16),
                    ((4, 16, FB), BF16),
                    ((4, 16, FB), BF16),
                    ((4, 16, FB), F32),
                    ((4, 16, FB), BF16),
                    ((NS, 16, FB), BF16),
                )
            ],
            pltpu.SMEM((2, 8), jnp.int32),
            pltpu.SMEM((2, 8), jnp.int32),
            pltpu.SMEM((8,), F32),
            pltpu.VMEM((2, 8, WL), BF16),
            pltpu.VMEM((8, 128), jnp.int32),
            pltpu.VMEM((1, HD), F32),
            *[pltpu.VMEM((1, WL), F32)] * 5,
            pltpu.SemaphoreType.DMA((23,)),
            pltpu.SemaphoreType.DMA((24,)),
            pltpu.SemaphoreType.DMA((24,)),
        ],
        compiler_params=pltpu.CompilerParams(
            collective_id=0, has_side_effects=True, vmem_limit_bytes=60 * 1024 * 1024
        ),
        name="decode_step",
    )(
        lengths, slot_owner, guidance, hidden, allowed_ids.reshape(8, 128), freq, *gains,
        query_weight, key_weight, value_weight, output_weight.T, gate_weight, up_weight, down_weight.T,
        embedding, cond_keys, cond_values, uncond_keys, uncond_values,
    )
    return base + lift


def solution(mesh):
    return jax.shard_map(
        on_device,
        mesh=mesh,
        in_specs=(
            P(None, None, ("guide", "seq")),
            P(),
            P(),
            P(("kv", "seq")),
            P(),
            P(("guide", "seq")),
            P(("guide", "seq")),
            P(("guide", "seq")),
            P(("guide", "seq")),
            P(("guide", "seq")),
            P(("guide", "seq"), "kv"),
            P(("guide", "seq"), "kv"),
            P(("guide", "seq"), "kv"),
            P("kv", ("guide", "seq")),
            P(("guide", "seq"), "kv"),
            P(("guide", "seq"), "kv"),
            P("kv", ("guide", "seq")),
            P(("kv", "seq"), "guide"),
            P(None, ("guide", "seq"), "kv"),
            P(None, ("guide", "seq"), "kv"),
            P(None, ("guide", "seq"), "kv"),
            P(None, ("guide", "seq"), "kv"),
        ),
        out_specs=P("guide", ("kv", "seq")),
        check_vma=False,
    )
```

```python
import functools

import jax
import jax.numpy as jnp
import numpy as np
from jax import lax
from jax.experimental import pallas as pl
from jax.experimental.pallas import tpu as pltpu
from jax.sharding import PartitionSpec as P

D = 4608
H = 32
HD = 128
EPS = 1e-06
ATTN_CAP = 50.0
LOGIT_CAP = 30.0
THETA = 10000.0
MESH = pl.DeviceIdType.MESH
F32 = jnp.float32
BF16 = jnp.bfloat16
NG, NKV, NS = 2, 4, 16
NP = NG * NS
WL = D // NP
FFL = 9216
FB = 256
EXTRA = 8
ROWS = 2048
HALF = D // 2
PICK = 1024


def iota(shape, dim):
    return lax.broadcasted_iota(jnp.int32, shape, dim)


def column_to_row(col):
    n = col.shape[0]
    spread = jnp.where(iota((n, 128), 0) == iota((n, 128), 1), jnp.broadcast_to(col, (n, 128)), 0.0)
    return jnp.sum(spread, axis=0, keepdims=True)


def row_to_column(row, n, first=0):
    lanes = iota((n, 128), 1)
    picked = jnp.where(lanes == iota((n, 128), 0) + first, jnp.broadcast_to(row, (n, 128)), 0.0)
    return jnp.sum(picked, axis=1, keepdims=True)


def nt_dot(a, b):
    return lax.dot_general(a, b, (((1,), (1,)), ((), ())), preferred_element_type=F32)


def nn_dot(a, b):
    return jnp.dot(a, b, preferred_element_type=F32)


def one_hot(mask):
    return jnp.where(mask, 1.0, 0.0).astype(BF16)


def step_kernel(
    lengths_h, owner_h, guidance_h, hidden_h, ids_h, freq_h, gain0_h, gain1_h, gain2_h, gain3_h, gain4_h,
    qw_h, kw_h, vw_h, ow_h, gw_h, uw_h, dw_h, emb_h, ck_h, cv_h, uk_h, uv_h,
    base_ref, lift_ref,
    w_qkv, w_o, w_g, w_u, w_d, emb, ck, cv, uk, uv,
    pick, table, qs, ks, vs, rows_f,
    s1, r1, b2, s3, r3, b4, b6, bm, act, b12, b13, b14, s16, r16,
    pa, qa, ka, sa, ra, ta, ua, va, wa, xa, pb, qb, kb, sb, rb, tb, ub, vb, wb, xb,
    lengths, owner, guidance, hidden, ids, freq, gain0, gain1, gain2, gain3, gain4,
    load_sem, send_sem, recv_sem,
):
    g = lax.axis_index("guide")
    kv = lax.axis_index("kv")
    s = lax.axis_index("seq")
    z = lax.div(s, 4)
    x = lax.rem(s, 4)
    me = g * NS + s

    loads = [
        pltpu.make_async_copy(src, dst, load_sem.at[i])
        for i, (src, dst) in enumerate(
            [
                (qw_h, w_qkv.at[:, pl.ds(0, 1024)]),
                (kw_h, w_qkv.at[:, pl.ds(1024, 512)]),
                (vw_h, w_qkv.at[:, pl.ds(1536, 512)]),
                (ck_h, ck),
                (uk_h, uk),
                (cv_h, cv),
                (uv_h, uv),
                (ow_h, w_o.at[kv]),
                (gw_h, w_g),
                (uw_h, w_u),
                (dw_h, w_d),
                (emb_h, emb),
                (hidden_h, hidden),
                (gain0_h, gain0),
                (lengths_h, lengths),
                (owner_h, owner),
                (guidance_h, guidance),
                (ids_h, ids),
                (freq_h, freq),
                (gain1_h, gain1),
                (gain2_h, gain2),
                (gain3_h, gain3),
                (gain4_h, gain4),
            ]
        )
    ]

    def peer(off):
        g2 = lax.rem(g + lax.div(off, 16), 2)
        z2 = lax.rem(z + lax.div(lax.rem(off, 16), 4), 4)
        x2 = lax.rem(x + lax.rem(off, 4), 4)
        return g2, z2 * 4 + x2

    def to_plane(body, count=NP):
        def one(off, carry):
            g2, s2 = peer(off)
            body(g2, s2)
            return carry

        lax.fori_loop(1, count, one, 0)

    def to_kv(body):
        for off in range(1, NKV):
            body(lax.rem(kv + off, NKV))

    def send(src, dst, i, device):
        pltpu.make_async_remote_copy(
            src_ref=src, dst_ref=dst, send_sem=send_sem.at[i], recv_sem=recv_sem.at[i],
            device_id=device, device_id_type=MESH,
        ).start()

    def whole(ref, i):
        return pltpu.make_async_remote_copy(
            src_ref=ref, dst_ref=ref, send_sem=send_sem.at[i], recv_sem=recv_sem.at[i],
            device_id={"guide": lax.rem(g + 1, 2)}, device_id_type=MESH,
        )

    pending = []

    def finish():
        for ref, i, when in pending:
            if when is None:
                whole(ref, i).wait_send()
            else:
                pl.when(when)(functools.partial(lambda ref, i: whole(ref, i).wait_send(), ref, i))

    barrier = pltpu.get_barrier_semaphore()
    to_plane(lambda g2, s2: pl.semaphore_signal(
        barrier, inc=1, device_id={"guide": g2, "seq": s2}, device_id_type=MESH))
    to_kv(lambda k2: pl.semaphore_signal(barrier, inc=1, device_id={"kv": k2}, device_id_type=MESH))

    for load in loads[12:23] + loads[0:3]:
        load.start()
    other = {"guide": lax.rem(g + 1, 2)}
    tail = NP * FB
    holds_extra = (lax.rem(x, 2) == lax.rem(z, 2)) & (lax.div(z, 2) == g)
    extra = 2 * z + lax.div(x, 2)
    set_a = (pa, qa, ka, sa, ra, ta, ua, va, wa, xa)
    set_b = (pb, qb, kb, sb, rb, tb, ub, vb, wb, xb)

    def ffw_product(rows, buffers, base):
        away, _, keep, _, _, tail_away, _, tail_keep, _, _ = buffers
        high = rows.astype(BF16)
        low = (rows - high.astype(F32)).astype(BF16)
        both = jnp.concatenate([high, low], axis=0)

        def product(weight, cols):
            wide = nn_dot(both, weight[:, cols])
            return wide[0:16, :] + wide[16:32, :]

        for whose, main, rest in ((1 - g, away, tail_away), (g, keep, tail_keep)):
            cols = pl.ds(pl.multiple_of(whose * (NS * FB), NS * FB), NS * FB)
            tail_cols = pl.ds(pl.multiple_of(tail + whose * 512, 512), 512)
            for at, weight in ((0, w_g), (1, w_u)):
                part = product(weight, cols).astype(main.dtype)
                for c in range(NS):
                    main[c, :, at * FB:(at + 1) * FB] = part[:, c * FB:(c + 1) * FB]
                part = product(weight, tail_cols).astype(rest.dtype)
                for c in range(4):
                    rest[c, :, at * 128:(at + 1) * 128] = part[:, c * 128:(c + 1) * 128]
            if main is away:
                send(away, buffers[1], base, other)
                send(tail_away, buffers[6], base + 1, other)
                pending.append((away, base, None))
                pending.append((tail_away, base + 1, None))

    def ffw_combine(buffers, base):
        _, came, keep, out, _, _, tail_came, tail_keep, tail_out, _ = buffers
        whole(came, base).wait_recv()
        whole(tail_came, base + 1).wait_recv()
        out[...] = (keep[...] + came[...].astype(F32)).astype(BF16)
        tail_out[...] = (tail_keep[...] + tail_came[...].astype(F32)).astype(BF16)

    def ffw_send(buffers, base):
        _, _, _, out, into, _, _, _, tail_out, tail_into = buffers

        def one(q, carry):
            z2 = 2 * g + lax.div(q, 2)
            s2 = 4 * z2 + 2 * lax.rem(q, 2) + lax.rem(z2, 2)

            @pl.when(s2 != s)
            def _():
                send(tail_out.at[q], tail_into.at[s], base + 1, {"seq": s2})

            return carry

        lax.fori_loop(0, 4, one, 0)
        to_plane(lambda g2, s2: send(out.at[s2], into.at[s], base, {"seq": s2}), NS)
        into[s] = out[s]
        pending.append((out.at[pl.ds(0, NS - 1)], base, None))
        pending.append((tail_out.at[pl.ds(0, 3)], base + 1, holds_extra))
        pending.append((tail_out, base + 1, jnp.logical_not(holds_extra)))

    for load in loads[12:23]:
        load.wait()
    x_in = hidden[...].astype(F32).reshape(16, WL)
    normed = (x_in * gain0[...]).astype(BF16)
    x_sq = column_to_row(jnp.sum(x_in * x_in, axis=-1, keepdims=True))
    for i in range(3):
        loads[i].wait()
    for i in (8, 9, 3, 4, 7, 5, 6, 11, 10):
        loads[i].start()
    part = nn_dot(normed, w_qkv[...])
    for j in range(NS):
        for k in range(NG):
            s1[k * NS + j, 0:8, :] = part[k * 8:(k + 1) * 8, j * 128:(j + 1) * 128]
            s1[k * NS + j, 8:9, :] = x_sq
    r1[me] = s1[me]

    first_row = (kv * NS + s) * ROWS

    def pick_rows(i, carry):
        base = pl.multiple_of(i * 256, 256)
        v = iota((256, 128), 0) + (first_row + base)
        for c in range(PICK // 128):
            pick[pl.ds(base, 256), c * 128:(c + 1) * 128] = one_hot(v == ids[c:c + 1, :])
        return carry

    def pick_table(first, count):
        def one(i, carry):
            cols = pl.ds(pl.multiple_of(i * 256, 256), 256)
            table[cols, :] = lax.dot_general(
                emb[:, cols], pick[...], (((0,), (0,)), ((), ())), preferred_element_type=F32
            ).astype(BF16)
            return carry

        lax.fori_loop(first, first + count, one, 0)

    turn_row = iota((8, 128), 0)
    position = jnp.zeros((8, 128), F32)
    for i in range(8):
        position = jnp.where(turn_row == i, lengths[g, i].astype(F32), position)
    angle = position * freq[...]
    cosine = jnp.cos(angle)
    sine = jnp.sin(angle)
    sine = jnp.where(iota((8, 128), 1) < 64, -sine, sine)
    pl.semaphore_wait(barrier, NP - 1 + NKV - 1)
    to_plane(lambda g2, s2: send(
        s1.at[g2 * NS + s2], r1.at[me], 0, {"guide": g2, "seq": s2}))
    pending.append((s1.at[pl.ds(0, NP - 1)], 0, None))

    loads[8].wait()
    loads[9].wait()
    ffw_product(x_in * gain2[...], set_a, 6)
    lax.fori_loop(0, ROWS // 256, pick_rows, 0)
    ffw_combine(set_a, 6)
    whole(r1.at[pl.ds(0, NP - 1)], 0).wait_recv()
    total = jnp.sum(r1[...], axis=0)
    scale = lax.rsqrt(row_to_column(total[8:9, :], 8, 8 * g) / D + EPS)
    y = total[0:8, :] * scale
    turned = y * cosine + pltpu.roll(y, 64, 1) * sine
    y = jnp.where(s < 12, turned, y)
    y = jnp.where(s < 8, y * (D // H) ** (-0.5), y)
    b2[me] = y.astype(BF16).astype(F32)
    to_plane(lambda g2, s2: send(b2.at[me], b2.at[me], 1, {"guide": g2, "seq": s2}))
    pending.append((b2.at[pl.ds(0, NP - 1)], 1, None))
    ffw_send(set_a, 17)
    loads[7].wait()
    to_kv(lambda k2: send(w_o.at[kv], w_o.at[kv], 4, {"kv": k2}))
    pending.append((w_o.at[pl.ds(0, NKV - 1)], 4, None))

    picks = []
    r_ = iota((64, 128), 0)
    c_ = iota((64, 128), 1)
    for k in range(NG):
        held = jnp.zeros((64, 128), jnp.int32)
        for j in range(8):
            held = jnp.where(lax.div(r_, 8) == j, owner[k, j], held)
        same = lax.rem(c_, 8) == held
        head = lax.rem(r_, 8)
        blk = lax.div(c_, 8)
        picks.append((
            one_hot(same & (blk == head)),
            one_hot(same & (blk == 8 + lax.div(head, 2))),
            one_hot(same & (blk == 12 + lax.div(head, 2))),
        ))
    block = me
    limits = []
    for k, span in ((0, 256), (1, 64)):
        limit = jnp.zeros((64, span), jnp.int32)
        row = lax.div(iota((64, span), 0), 8)
        for j in range(8):
            limit = jnp.where(row == j, lengths[k, owner[k, j]], limit)
        limits.append(iota((64, span), 1) + block * span < limit)

    for i in range(3, 7):
        loads[i].wait()
    whole(b2.at[pl.ds(0, NP - 1)], 1).wait_recv()
    gathered = b2[...].reshape(NG, 128, 128).astype(BF16)
    lane_head = lax.div(lax.rem(iota((64, 128), 0), 8), 2)
    for k, span, keys, values in ((0, 256, ck, cv), (1, 64, uk, uv)):
        q = nn_dot(picks[k][0], gathered[k])
        for j in range(8):
            qs[k * 8 + j] = q[j * 8:(j + 1) * 8, :]
        wide = [jnp.where(lane_head == b, q, 0.0) for b in range(4)]
        scores = []
        for j in range(8):
            qj = jnp.concatenate([w[j * 8:(j + 1) * 8, :] for w in wide], axis=1).astype(BF16)
            scores.append(nt_dot(qj, keys[j]))
        score = jnp.concatenate(scores, axis=0)
        prob = jnp.where(limits[k], jnp.exp(ATTN_CAP * jnp.tanh(score / ATTN_CAP)), 0.0)
        denom = jnp.sum(prob, axis=1, keepdims=True)
        for j in range(8):
            pj = prob[j * 8:(j + 1) * 8, :].astype(BF16)
            full = nn_dot(pj, values[j])
            mine = jnp.zeros((8, 128), F32)
            for b in range(4):
                mine = jnp.where(lane_head[0:8, :] == b, full[:, b * 128:(b + 1) * 128], mine)
            s3[k * 8 + j, 0:8, :] = mine
            s3[k * 8 + j, 8:9, :] = column_to_row(denom[j * 8:(j + 1) * 8, :])

    tile_guide = lax.rem(s, 2)
    holds_tile = g == tile_guide

    def send_tile(off, carry):
        i = lax.rem(s + off, NS)
        send(s3.at[i], r3.at[me], 2, {"guide": lax.rem(i, 2), "seq": i})
        return carry

    lax.fori_loop(1, NS, send_tile, 0)

    @pl.when(jnp.logical_not(holds_tile))
    def _():
        send(s3.at[s], r3.at[me], 2, {"guide": tile_guide, "seq": s})

    pending.append((s3.at[pl.ds(0, NS - 1)], 2, holds_tile))
    pending.append((s3, 2, jnp.logical_not(holds_tile)))
    pending.append((table.at[pl.ds(0, (NP * NKV - 1) * 8), pl.ds(0, 128)], 3, holds_tile))

    for k in range(NG):
        kx = nn_dot(picks[k][1], gathered[k])
        vx = nn_dot(picks[k][2], gathered[k])
        for j in range(8):
            ks[k * 8 + j] = kx[j * 8:(j + 1) * 8, :]
            vs[k * 8 + j] = vx[j * 8:(j + 1) * 8, :]

    loads[11].wait()
    pick_table(0, 1)

    @pl.when(holds_tile)
    def _():
        r3[me] = s3[s]
        own = jnp.exp(ATTN_CAP * jnp.tanh(jnp.sum(qs[s] * ks[s], axis=1, keepdims=True) / ATTN_CAP))
        whole(r3.at[pl.ds(0, NP - 1)], 2).wait_recv()
        sums = jnp.sum(r3[...], axis=0)
        numer = sums[0:8, :] + own.astype(BF16).astype(F32) * vs[s]
        den = row_to_column(sums[8:9, :], 8) + own
        at = kv * NS + s
        b4[at] = (numer / den).astype(BF16)

        def to_all(off, carry):
            g2, s2 = peer(lax.rem(off, NP))
            k2 = lax.rem(kv + lax.div(off, NP), NKV)
            send(b4.at[at], b4.at[at], 3, {"guide": g2, "kv": k2, "seq": s2})
            return carry

        lax.fori_loop(1, NP * NKV, to_all, 0)

    r_ = iota((128, 128), 0)
    c_ = iota((128, 128), 1)
    held = jnp.zeros((128, 128), jnp.int32)
    for i in range(16):
        held = jnp.where(lax.div(c_, 8) == i, owner[i // 8, i % 8], held)
    back = one_hot(
        (lax.div(r_, 16) == lax.rem(c_, 8))
        & (lax.rem(lax.div(r_, 8), 2) == lax.div(c_, 64))
        & (lax.rem(r_, 8) == held)
    )
    pick_table(1, 3)
    whole(w_o.at[pl.ds(0, NKV - 1)], 4).wait_recv()

    @pl.when(holds_tile)
    def _():
        whole(b4.at[pl.ds(0, NKV * NS - 1)], 3).wait_recv()

    @pl.when(jnp.logical_not(holds_tile))
    def _():
        whole(b4, 3).wait_recv()

    projected = jnp.zeros((16, WL), F32)
    for k in range(NKV):
        tiles = b4[k * NS:(k + 1) * NS].astype(F32).reshape(128, 128).astype(BF16)
        att = nn_dot(back, tiles)
        att = jnp.concatenate([att[h * 16:(h + 1) * 16, :] for h in range(8)], axis=1).astype(BF16)
        projected = projected + nt_dot(att, w_o[k])
    branch = projected * gain1[...]
    ffw_product(branch * gain2[...], set_b, 19)
    b6[me, 0:1, :] = column_to_row(jnp.sum(projected * projected, axis=-1, keepdims=True))
    b6[me, 1:2, :] = column_to_row(jnp.sum(x_in * branch, axis=-1, keepdims=True))
    b6[me, 2:3, :] = column_to_row(jnp.sum(branch * branch, axis=-1, keepdims=True))
    b6[me, 3:4, :] = x_sq
    to_plane(lambda g2, s2: send(b6.at[me], b6.at[me], 5, {"guide": g2, "seq": s2}))
    pending.append((b6.at[pl.ds(0, NP - 1)], 5, None))
    ffw_combine(set_b, 19)
    ffw_send(set_b, 21)
    pick_table(4, 3)
    whole(b6.at[pl.ds(0, NP - 1)], 5).wait_recv()
    sums = jnp.sum(b6[...], axis=0)
    out_scale = lax.rsqrt(row_to_column(sums[0:1, :], 16) / D + EPS)
    middle_sq = (
        row_to_column(sums[3:4, :], 16)
        + 2.0 * out_scale * row_to_column(sums[1:2, :], 16)
        + out_scale * out_scale * row_to_column(sums[2:3, :], 16)
    )
    ffw_scale = lax.rsqrt(jnp.maximum(middle_sq, 0.0) / D + EPS)
    bm[s, 0:16, :] = x_in + branch * out_scale
    bm[s, 16:17, :] = gain3[...]
    bm[s, 17:18, :] = gain4[...]

    def activate(first, second):
        n = first.shape[1] // 2
        both = (first + out_scale * second) * ffw_scale
        return (jax.nn.gelu(both[:, 0:n], approximate=True) * both[:, n:2 * n]).astype(BF16)

    def gathered_sum(ref):
        return jnp.sum(ref[...].astype(F32), axis=0)

    whole(ra.at[pl.ds(0, NS - 1)], 17).wait_recv()
    first = gathered_sum(ra)
    whole(rb.at[pl.ds(0, NS - 1)], 21).wait_recv()
    mine = pl.ds(pl.multiple_of(me * FB, FB), FB)
    act[:, mine] = activate(first, gathered_sum(rb))
    to_plane(lambda g2, s2: send(act.at[:, mine], act.at[:, mine], 10, {"guide": g2, "seq": s2}))
    pending.append((act.at[:, pl.ds(0, (NP - 1) * FB)], 10, None))
    pending.append((act.at[:, pl.ds(0, (NP - 1) * 128)], 11, holds_extra))

    @pl.when(holds_extra)
    def _():
        own = extra - 4 * g
        xa[s] = wa[own]
        xb[s] = wb[own]
        whole(xa.at[pl.ds(0, NS - 1)], 18).wait_recv()
        whole(xb.at[pl.ds(0, NS - 1)], 22).wait_recv()
        cols = pl.ds(pl.multiple_of(tail + extra * 128, 128), 128)
        act[:, cols] = activate(gathered_sum(xa), gathered_sum(xb))
        to_plane(lambda g2, s2: send(act.at[:, cols], act.at[:, cols], 11, {"guide": g2, "seq": s2}))

    pick_table(7, 2)
    loads[10].wait()
    whole(act.at[:, pl.ds(0, (NP - 1) * FB)], 10).wait_recv()

    @pl.when(holds_extra)
    def _():
        whole(act.at[:, pl.ds(0, (EXTRA - 1) * 128)], 11).wait_recv()

    @pl.when(jnp.logical_not(holds_extra))
    def _():
        whole(act.at[:, pl.ds(0, EXTRA * 128)], 11).wait_recv()

    to_plane(lambda g2, s2: send(bm.at[s], bm.at[s], 9, {"seq": s2}), NS)
    pending.append((bm.at[pl.ds(0, NS - 1)], 9, None))
    b12[kv] = nt_dot(act[...], w_d[...])
    to_kv(lambda k2: send(b12.at[kv], b12.at[kv], 12, {"kv": k2}))
    pending.append((b12.at[pl.ds(0, NKV - 1)], 12, None))
    whole(b12.at[pl.ds(0, NKV - 1)], 12).wait_recv()
    ffw_out = (b12[0] + b12[1]) + (b12[2] + b12[3])
    b14[s] = ffw_out.astype(BF16)
    b13[me] = column_to_row(jnp.sum(ffw_out * ffw_out, axis=-1, keepdims=True))
    to_plane(lambda g2, s2: send(b14.at[s], b14.at[s], 14, {"seq": s2}), NS)
    pending.append((b14.at[pl.ds(0, NS - 1)], 14, None))
    to_plane(lambda g2, s2: send(b13.at[me], b13.at[me], 13, {"guide": g2, "seq": s2}))
    pending.append((b13.at[pl.ds(0, NP - 1)], 13, None))

    whole(bm.at[pl.ds(0, NS - 1)], 9).wait_recv()
    whole(b13.at[pl.ds(0, NP - 1)], 13).wait_recv()
    branch_scale = lax.rsqrt(row_to_column(jnp.sum(b13[...], axis=0), 16) / D + EPS)
    whole(b14.at[pl.ds(0, NS - 1)], 14).wait_recv()
    last_sq = jnp.zeros((16, WL), F32)
    for t in range(NS):
        last = bm[t, 0:16, :] + b14[t].astype(F32) * branch_scale * bm[t, 16:17, :]
        last_sq = last_sq + last * last
        rows_f[:, t * WL:(t + 1) * WL] = last * bm[t, 17:18, :]
    sq_row = column_to_row(jnp.sum(last_sq, axis=-1, keepdims=True))

    logit = nn_dot(rows_f[...].astype(BF16), table[...])
    lower = jnp.concatenate([logit[0:4, :], logit[8:12, :]], axis=0)
    upper = jnp.concatenate([logit[4:8, :], logit[12:16, :]], axis=0)
    s16[0:8, :] = jnp.where(g == 0, upper, lower)
    s16[8:9, 0:128] = sq_row
    send(s16, r16, 16, other)
    pending.append((s16, 16, None))
    keep = jnp.where(g == 0, lower, upper)
    whole(r16, 16).wait_recv()
    lanes = iota((8, 128), 1)
    rowi = iota((8, 128), 0)
    want = lax.div(rowi, 4) * 8 + 4 * g + lax.rem(rowi, 4)
    sq = jnp.sum(jnp.where(lanes == want, jnp.broadcast_to(sq_row + r16[8:9, 0:128], (8, 128)), 0.0),
                 axis=1, keepdims=True)
    final_scale = lax.rsqrt(sq / D + EPS)
    share = jnp.zeros((4, 1), F32)
    for i in range(4):
        share = jnp.where(iota((4, 1), 0) == i, guidance[4 * g + i], share)
    capped = LOGIT_CAP * jnp.tanh((keep + r16[0:8, :]) * final_scale / LOGIT_CAP)
    base_ref[...] = capped[4:8, :]
    lift_ref[...] = share * (capped[0:4, :] - capped[4:8, :])

    finish()


def on_device(
    hidden, lengths, slot_owner, allowed_ids, guidance,
    pre_attn_gain, post_attn_gain, pre_ffw_gain, post_ffw_gain, final_gain,
    query_weight, key_weight, value_weight, output_weight,
    gate_weight, up_weight, down_weight, embedding,
    cond_keys, cond_values, uncond_keys, uncond_values,
):
    lane = np.arange(HD) % (HD // 2)
    freq = jnp.asarray((THETA ** (-2.0 * lane / HD)).astype(np.float32).reshape(1, HD))
    gains = [
        gain.reshape(1, WL)
        for gain in (pre_attn_gain, post_attn_gain, pre_ffw_gain, post_ffw_gain, final_gain)
    ]
    vmem = pl.BlockSpec(memory_space=pltpu.VMEM)
    hbm = pl.BlockSpec(memory_space=pl.ANY)
    base, lift = pl.pallas_call(
        step_kernel,
        out_shape=[jax.ShapeDtypeStruct((4, PICK), F32)] * 2,
        in_specs=[hbm] * 23,
        out_specs=[vmem] * 2,
        scratch_shapes=[
            pltpu.VMEM((WL, 2048), BF16),
            pltpu.VMEM((NKV, WL, 1024), BF16),
            pltpu.VMEM((WL, FFL), BF16),
            pltpu.VMEM((WL, FFL), BF16),
            pltpu.VMEM((WL, FFL), BF16),
            pltpu.VMEM((ROWS, HALF), BF16),
            pltpu.VMEM((8, 256, 512), BF16),
            pltpu.VMEM((8, 256, 512), BF16),
            pltpu.VMEM((8, 64, 512), BF16),
            pltpu.VMEM((8, 64, 512), BF16),
            pltpu.VMEM((ROWS, PICK), BF16),
            pltpu.VMEM((HALF, PICK), BF16),
            pltpu.VMEM((16, 8, 128), F32),
            pltpu.VMEM((16, 8, 128), F32),
            pltpu.VMEM((16, 8, 128), F32),
            pltpu.VMEM((16, HALF), F32),
            pltpu.VMEM((NP, 9, 128), F32),
            pltpu.VMEM((NP, 9, 128), F32),
            pltpu.VMEM((NP, 8, 128), F32),
            pltpu.VMEM((16, 9, 128), F32),
            pltpu.VMEM((NP, 9, 128), F32),
            pltpu.VMEM((NKV * NS, 8, 128), BF16),
            pltpu.VMEM((NP, 4, 128), F32),
            pltpu.VMEM((NS, 18, WL), F32),
            pltpu.VMEM((16, FFL), BF16),
            pltpu.VMEM((NKV, 16, WL), F32),
            pltpu.VMEM((NP, 1, 128), F32),
            pltpu.VMEM((NS, 16, WL), BF16),
            pltpu.VMEM((9, PICK), F32),
            pltpu.VMEM((9, PICK), F32),
            *[
                pltpu.VMEM(shape, kind)
                for _ in range(2)
                for shape, kind in (
                    ((NS, 16, 2 * FB), BF16),
                    ((NS, 16, 2 * FB), BF16),
                    ((NS, 16, 2 * FB), F32),
                    ((NS, 16, 2 * FB), BF16),
                    ((NS, 16, 2 * FB), BF16),
                    ((4, 16, FB), BF16),
                    ((4, 16, FB), BF16),
                    ((4, 16, FB), F32),
                    ((4, 16, FB), BF16),
                    ((NS, 16, FB), BF16),
                )
            ],
            pltpu.SMEM((2, 8), jnp.int32),
            pltpu.SMEM((2, 8), jnp.int32),
            pltpu.SMEM((8,), F32),
            pltpu.VMEM((2, 8, WL), BF16),
            pltpu.VMEM((8, 128), jnp.int32),
            pltpu.VMEM((1, HD), F32),
            *[pltpu.VMEM((1, WL), F32)] * 5,
            pltpu.SemaphoreType.DMA((23,)),
            pltpu.SemaphoreType.DMA((24,)),
            pltpu.SemaphoreType.DMA((24,)),
        ],
        compiler_params=pltpu.CompilerParams(
            collective_id=0, has_side_effects=True, vmem_limit_bytes=60 * 1024 * 1024
        ),
        name="decode_step",
    )(
        lengths, slot_owner, guidance, hidden, allowed_ids.reshape(8, 128), freq, *gains,
        query_weight, key_weight, value_weight, output_weight.T, gate_weight, up_weight, down_weight.T,
        embedding, cond_keys, cond_values, uncond_keys, uncond_values,
    )
    return base + lift


def solution(mesh):
    return jax.shard_map(
        on_device,
        mesh=mesh,
        in_specs=(
            P(None, None, ("guide", "seq")),
            P(),
            P(),
            P(("kv", "seq")),
            P(),
            P(("guide", "seq")),
            P(("guide", "seq")),
            P(("guide", "seq")),
            P(("guide", "seq")),
            P(("guide", "seq")),
            P(("guide", "seq"), "kv"),
            P(("guide", "seq"), "kv"),
            P(("guide", "seq"), "kv"),
            P("kv", ("guide", "seq")),
            P(("guide", "seq"), "kv"),
            P(("guide", "seq"), "kv"),
            P("kv", ("guide", "seq")),
            P(("kv", "seq"), "guide"),
            P(None, ("guide", "seq"), "kv"),
            P(None, ("guide", "seq"), "kv"),
            P(None, ("guide", "seq"), "kv"),
            P(None, ("guide", "seq"), "kv"),
        ),
        out_specs=P("guide", ("kv", "seq")),
        check_vma=False,
    )
```

```python
import functools

import jax
import jax.numpy as jnp
import numpy as np
from jax import lax
from jax.experimental import pallas as pl
from jax.experimental.pallas import tpu as pltpu
from jax.sharding import PartitionSpec as P

D = 4608
H = 32
HD = 128
EPS = 1e-06
ATTN_CAP = 50.0
LOGIT_CAP = 30.0
THETA = 10000.0
MESH = pl.DeviceIdType.MESH
F32 = jnp.float32
BF16 = jnp.bfloat16
NG, NKV, NS = 2, 4, 16
NP = NG * NS
WL = D // NP
FFL = 9216
FB = 256
EXTRA = 8
ROWS = 2048
HALF = D // 2
PICK = 1024


def iota(shape, dim):
    return lax.broadcasted_iota(jnp.int32, shape, dim)


def column_to_row(col):
    n = col.shape[0]
    spread = jnp.where(iota((n, 128), 0) == iota((n, 128), 1), jnp.broadcast_to(col, (n, 128)), 0.0)
    return jnp.sum(spread, axis=0, keepdims=True)


def row_to_column(row, n, first=0):
    lanes = iota((n, 128), 1)
    picked = jnp.where(lanes == iota((n, 128), 0) + first, jnp.broadcast_to(row, (n, 128)), 0.0)
    return jnp.sum(picked, axis=1, keepdims=True)


def nt_dot(a, b):
    return lax.dot_general(a, b, (((1,), (1,)), ((), ())), preferred_element_type=F32)


def nn_dot(a, b):
    return jnp.dot(a, b, preferred_element_type=F32)


def one_hot(mask):
    return jnp.where(mask, 1.0, 0.0).astype(BF16)


def step_kernel(
    lengths_h, owner_h, guidance_h, hidden_h, ids_h, freq_h, gain0_h, gain1_h, gain2_h, gain3_h, gain4_h,
    qw_h, kw_h, vw_h, ow_h, gw_h, uw_h, dw_h, emb_h, ck_h, cv_h, uk_h, uv_h,
    base_ref, lift_ref,
    w_qkv, w_o, w_g, w_u, w_d, emb, ck, cv, uk, uv,
    pick, table, qs, ks, vs, rows_f,
    s1, r1, b2, s3, r3, b4, b5, b6, bm, act, b12, b13, b14, s16, r16,
    pa, qa, ka, sa, ra, ta, ua, va, wa, xa, pb, qb, kb, sb, rb, tb, ub, vb, wb, xb,
    lengths, owner, guidance, hidden, ids, freq, gain0, gain1, gain2, gain3, gain4,
    load_sem, send_sem, recv_sem,
):
    g = lax.axis_index("guide")
    kv = lax.axis_index("kv")
    s = lax.axis_index("seq")
    z = lax.div(s, 4)
    x = lax.rem(s, 4)
    me = g * NS + s

    loads = [
        pltpu.make_async_copy(src, dst, load_sem.at[i])
        for i, (src, dst) in enumerate(
            [
                (qw_h, w_qkv.at[:, pl.ds(0, 1024)]),
                (kw_h, w_qkv.at[:, pl.ds(1024, 512)]),
                (vw_h, w_qkv.at[:, pl.ds(1536, 512)]),
                (ck_h, ck),
                (uk_h, uk),
                (cv_h, cv),
                (uv_h, uv),
                (ow_h, w_o),
                (gw_h, w_g),
                (uw_h, w_u),
                (dw_h, w_d),
                (emb_h, emb),
                (hidden_h, hidden),
                (gain0_h, gain0),
                (lengths_h, lengths),
                (owner_h, owner),
                (guidance_h, guidance),
                (ids_h, ids),
                (freq_h, freq),
                (gain1_h, gain1),
                (gain2_h, gain2),
                (gain3_h, gain3),
                (gain4_h, gain4),
            ]
        )
    ]

    def peer(off):
        g2 = lax.rem(g + lax.div(off, 16), 2)
        z2 = lax.rem(z + lax.div(lax.rem(off, 16), 4), 4)
        x2 = lax.rem(x + lax.rem(off, 4), 4)
        return g2, z2 * 4 + x2

    def to_plane(body, count=NP):
        def one(off, carry):
            g2, s2 = peer(off)
            body(g2, s2)
            return carry

        lax.fori_loop(1, count, one, 0)

    def to_kv(body):
        for off in range(1, NKV):
            body(lax.rem(kv + off, NKV))

    def send(src, dst, i, device):
        pltpu.make_async_remote_copy(
            src_ref=src, dst_ref=dst, send_sem=send_sem.at[i], recv_sem=recv_sem.at[i],
            device_id=device, device_id_type=MESH,
        ).start()

    def whole(ref, i):
        return pltpu.make_async_remote_copy(
            src_ref=ref, dst_ref=ref, send_sem=send_sem.at[i], recv_sem=recv_sem.at[i],
            device_id={"guide": lax.rem(g + 1, 2)}, device_id_type=MESH,
        )

    pending = []

    def finish():
        for ref, i, when in pending:
            if when is None:
                whole(ref, i).wait_send()
            else:
                pl.when(when)(functools.partial(lambda ref, i: whole(ref, i).wait_send(), ref, i))

    barrier = pltpu.get_barrier_semaphore()
    to_plane(lambda g2, s2: pl.semaphore_signal(
        barrier, inc=1, device_id={"guide": g2, "seq": s2}, device_id_type=MESH))
    to_kv(lambda k2: pl.semaphore_signal(barrier, inc=1, device_id={"kv": k2}, device_id_type=MESH))

    for load in loads[12:23] + loads[0:3]:
        load.start()
    other = {"guide": lax.rem(g + 1, 2)}
    tail = NP * FB
    holds_extra = (lax.rem(x, 2) == lax.rem(z, 2)) & (lax.div(z, 2) == g)
    extra = 2 * z + lax.div(x, 2)
    set_a = (pa, qa, ka, sa, ra, ta, ua, va, wa, xa)
    set_b = (pb, qb, kb, sb, rb, tb, ub, vb, wb, xb)

    def ffw_product(rows, buffers, base):
        away, _, keep, _, _, tail_away, _, tail_keep, _, _ = buffers
        high = rows.astype(BF16)
        low = (rows - high.astype(F32)).astype(BF16)
        both = jnp.concatenate([high, low], axis=0)

        def product(weight, cols):
            wide = nn_dot(both, weight[:, cols])
            return wide[0:16, :] + wide[16:32, :]

        for whose, main, rest in ((1 - g, away, tail_away), (g, keep, tail_keep)):
            cols = pl.ds(pl.multiple_of(whose * (NS * FB), NS * FB), NS * FB)
            tail_cols = pl.ds(pl.multiple_of(tail + whose * 512, 512), 512)
            for at, weight in ((0, w_g), (1, w_u)):
                part = product(weight, cols).astype(main.dtype)
                for c in range(NS):
                    main[c, :, at * FB:(at + 1) * FB] = part[:, c * FB:(c + 1) * FB]
                part = product(weight, tail_cols).astype(rest.dtype)
                for c in range(4):
                    rest[c, :, at * 128:(at + 1) * 128] = part[:, c * 128:(c + 1) * 128]
            if main is away:
                send(away, buffers[1], base, other)
                send(tail_away, buffers[6], base + 1, other)
                pending.append((away, base, None))
                pending.append((tail_away, base + 1, None))

    def ffw_combine(buffers, base):
        _, came, keep, out, _, _, tail_came, tail_keep, tail_out, _ = buffers
        whole(came, base).wait_recv()
        whole(tail_came, base + 1).wait_recv()
        out[...] = (keep[...] + came[...].astype(F32)).astype(BF16)
        tail_out[...] = (tail_keep[...] + tail_came[...].astype(F32)).astype(BF16)

    def ffw_send(buffers, base):
        _, _, _, out, into, _, _, _, tail_out, tail_into = buffers

        def one(q, carry):
            z2 = 2 * g + lax.div(q, 2)
            s2 = 4 * z2 + 2 * lax.rem(q, 2) + lax.rem(z2, 2)

            @pl.when(s2 != s)
            def _():
                send(tail_out.at[q], tail_into.at[s], base + 1, {"seq": s2})

            return carry

        lax.fori_loop(0, 4, one, 0)
        to_plane(lambda g2, s2: send(out.at[s2], into.at[s], base, {"seq": s2}), NS)
        into[s] = out[s]
        pending.append((out.at[pl.ds(0, NS - 1)], base, None))
        pending.append((tail_out.at[pl.ds(0, 3)], base + 1, holds_extra))
        pending.append((tail_out, base + 1, jnp.logical_not(holds_extra)))

    for load in loads[12:23]:
        load.wait()
    x_in = hidden[...].astype(F32).reshape(16, WL)
    normed = (x_in * gain0[...]).astype(BF16)
    x_sq = column_to_row(jnp.sum(x_in * x_in, axis=-1, keepdims=True))
    for i in range(3):
        loads[i].wait()
    for load in loads[3:12]:
        load.start()
    part = nn_dot(normed, w_qkv[...])
    for j in range(NS):
        for k in range(NG):
            s1[k * NS + j, 0:8, :] = part[k * 8:(k + 1) * 8, j * 128:(j + 1) * 128]
            s1[k * NS + j, 8:9, :] = x_sq
    r1[me] = s1[me]

    first_row = (kv * NS + s) * ROWS

    def pick_rows(i, carry):
        base = pl.multiple_of(i * 256, 256)
        v = iota((256, 128), 0) + (first_row + base)
        for c in range(PICK // 128):
            pick[pl.ds(base, 256), c * 128:(c + 1) * 128] = one_hot(v == ids[c:c + 1, :])
        return carry

    def pick_table(first, count):
        def one(i, carry):
            cols = pl.ds(pl.multiple_of(i * 256, 256), 256)
            table[cols, :] = lax.dot_general(
                emb[:, cols], pick[...], (((0,), (0,)), ((), ())), preferred_element_type=F32
            ).astype(BF16)
            return carry

        lax.fori_loop(first, first + count, one, 0)

    turn_row = iota((8, 128), 0)
    position = jnp.zeros((8, 128), F32)
    for i in range(8):
        position = jnp.where(turn_row == i, lengths[g, i].astype(F32), position)
    angle = position * freq[...]
    cosine = jnp.cos(angle)
    sine = jnp.sin(angle)
    sine = jnp.where(iota((8, 128), 1) < 64, -sine, sine)
    pl.semaphore_wait(barrier, NP - 1 + NKV - 1)
    to_plane(lambda g2, s2: send(
        s1.at[g2 * NS + s2], r1.at[me], 0, {"guide": g2, "seq": s2}))
    pending.append((s1.at[pl.ds(0, NP - 1)], 0, None))

    lax.fori_loop(0, ROWS // 256, pick_rows, 0)
    whole(r1.at[pl.ds(0, NP - 1)], 0).wait_recv()
    total = jnp.sum(r1[...], axis=0)
    scale = lax.rsqrt(row_to_column(total[8:9, :], 8, 8 * g) / D + EPS)
    y = total[0:8, :] * scale
    turned = y * cosine + pltpu.roll(y, 64, 1) * sine
    y = jnp.where(s < 12, turned, y)
    y = jnp.where(s < 8, y * (D // H) ** (-0.5), y)
    b2[me] = y.astype(BF16)
    to_plane(lambda g2, s2: send(b2.at[me], b2.at[me], 1, {"guide": g2, "seq": s2}))
    pending.append((b2.at[pl.ds(0, NP - 1)], 1, None))

    picks = []
    r_ = iota((64, 128), 0)
    c_ = iota((64, 128), 1)
    for k in range(NG):
        held = jnp.zeros((64, 128), jnp.int32)
        for j in range(8):
            held = jnp.where(lax.div(r_, 8) == j, owner[k, j], held)
        same = lax.rem(c_, 8) == held
        head = lax.rem(r_, 8)
        blk = lax.div(c_, 8)
        picks.append((
            one_hot(same & (blk == head)),
            one_hot(same & (blk == 8 + lax.div(head, 2))),
            one_hot(same & (blk == 12 + lax.div(head, 2))),
        ))
    block = me
    limits = []
    for k, span in ((0, 256), (1, 64)):
        limit = jnp.zeros((64, span), jnp.int32)
        row = lax.div(iota((64, span), 0), 8)
        for j in range(8):
            limit = jnp.where(row == j, lengths[k, owner[k, j]], limit)
        limits.append(iota((64, span), 1) + block * span < limit)

    loads[8].wait()
    loads[9].wait()
    ffw_product(x_in * gain2[...], set_a, 6)
    for i in range(3, 7):
        loads[i].wait()
    whole(b2.at[pl.ds(0, NP - 1)], 1).wait_recv()
    gathered = b2[...].astype(F32).reshape(NG, 128, 128).astype(BF16)
    lane_head = lax.div(lax.rem(iota((64, 128), 0), 8), 2)
    holds_tile = g == lax.rem(s, 2)

    def send_tiles(first):
        def one(off, carry):
            i = first + lax.rem(s + off, 8)

            @pl.when(jnp.logical_or(i != s, jnp.logical_not(holds_tile)))
            def _():
                send(s3.at[i], r3.at[me], 2, {"guide": lax.rem(i, 2), "seq": i})

            return carry

        lax.fori_loop(0, 8, one, 0)

    for k, span, keys, values in ((0, 256, ck, cv), (1, 64, uk, uv)):
        q = nn_dot(picks[k][0], gathered[k])
        for j in range(8):
            qs[k * 8 + j] = q[j * 8:(j + 1) * 8, :]
        wide = [jnp.where(lane_head == b, q, 0.0) for b in range(4)]
        scores = []
        for j in range(8):
            qj = jnp.concatenate([w[j * 8:(j + 1) * 8, :] for w in wide], axis=1).astype(BF16)
            scores.append(nt_dot(qj, keys[j]))
        score = jnp.concatenate(scores, axis=0)
        prob = jnp.where(limits[k], jnp.exp(ATTN_CAP * jnp.tanh(score / ATTN_CAP)), 0.0)
        denom = jnp.sum(prob, axis=1, keepdims=True)
        for j in range(8):
            pj = prob[j * 8:(j + 1) * 8, :].astype(BF16)
            full = nn_dot(pj, values[j])
            mine = jnp.zeros((8, 128), F32)
            for b in range(4):
                mine = jnp.where(lane_head[0:8, :] == b, full[:, b * 128:(b + 1) * 128], mine)
            s3[k * 8 + j, 0:8, :] = mine
            s3[k * 8 + j, 8:9, :] = column_to_row(denom[j * 8:(j + 1) * 8, :])
        send_tiles(k * 8)

    pending.append((s3.at[pl.ds(0, NS - 1)], 2, holds_tile))
    pending.append((s3, 2, jnp.logical_not(holds_tile)))
    pending.append((b2.at[pl.ds(0, NP - 1)], 3, holds_tile))

    for k in range(NG):
        kx = nn_dot(picks[k][1], gathered[k])
        vx = nn_dot(picks[k][2], gathered[k])
        for j in range(8):
            ks[k * 8 + j] = kx[j * 8:(j + 1) * 8, :]
            vs[k * 8 + j] = vx[j * 8:(j + 1) * 8, :]

    ffw_combine(set_a, 6)
    loads[11].wait()
    pick_table(0, 1)

    @pl.when(holds_tile)
    def _():
        r3[me] = s3[s]
        own = jnp.exp(ATTN_CAP * jnp.tanh(jnp.sum(qs[s] * ks[s], axis=1, keepdims=True) / ATTN_CAP))
        whole(r3.at[pl.ds(0, NP - 1)], 2).wait_recv()
        sums = jnp.sum(r3[...], axis=0)
        numer = sums[0:8, :] + own.astype(BF16).astype(F32) * vs[s]
        den = row_to_column(sums[8:9, :], 8) + own
        b4[s] = (numer / den).astype(BF16)
        to_plane(lambda g2, s2: send(b4.at[s], b4.at[s], 3, {"guide": g2, "seq": s2}))

    r_ = iota((128, 128), 0)
    c_ = iota((128, 128), 1)
    held = jnp.zeros((128, 128), jnp.int32)
    for i in range(16):
        held = jnp.where(lax.div(c_, 8) == i, owner[i // 8, i % 8], held)
    back = one_hot(
        (lax.div(r_, 16) == lax.rem(c_, 8))
        & (lax.rem(lax.div(r_, 8), 2) == lax.div(c_, 64))
        & (lax.rem(r_, 8) == held)
    )
    pick_table(1, 2)
    loads[7].wait()

    @pl.when(holds_tile)
    def _():
        whole(b4.at[pl.ds(0, NS - 1)], 3).wait_recv()

    @pl.when(jnp.logical_not(holds_tile))
    def _():
        whole(b4, 3).wait_recv()

    att = nn_dot(back, b4[...].astype(F32).reshape(128, 128).astype(BF16))
    att = jnp.concatenate([att[h * 16:(h + 1) * 16, :] for h in range(8)], axis=1).astype(BF16)
    b5[kv] = nt_dot(att, w_o[...])
    to_kv(lambda k2: send(b5.at[kv], b5.at[kv], 4, {"kv": k2}))
    pending.append((b5.at[pl.ds(0, NKV - 1)], 4, None))
    ffw_send(set_a, 17)
    pick_table(3, 1)
    whole(b5.at[pl.ds(0, NKV - 1)], 4).wait_recv()
    projected = (b5[0] + b5[1]) + (b5[2] + b5[3])
    branch = projected * gain1[...]
    ffw_product(branch * gain2[...], set_b, 19)
    b6[me, 0:1, :] = column_to_row(jnp.sum(projected * projected, axis=-1, keepdims=True))
    b6[me, 1:2, :] = column_to_row(jnp.sum(x_in * branch, axis=-1, keepdims=True))
    b6[me, 2:3, :] = column_to_row(jnp.sum(branch * branch, axis=-1, keepdims=True))
    b6[me, 3:4, :] = x_sq
    to_plane(lambda g2, s2: send(b6.at[me], b6.at[me], 5, {"guide": g2, "seq": s2}))
    pending.append((b6.at[pl.ds(0, NP - 1)], 5, None))
    ffw_combine(set_b, 19)
    ffw_send(set_b, 21)
    pick_table(4, 3)
    whole(b6.at[pl.ds(0, NP - 1)], 5).wait_recv()
    sums = jnp.sum(b6[...], axis=0)
    out_scale = lax.rsqrt(row_to_column(sums[0:1, :], 16) / D + EPS)
    middle_sq = (
        row_to_column(sums[3:4, :], 16)
        + 2.0 * out_scale * row_to_column(sums[1:2, :], 16)
        + out_scale * out_scale * row_to_column(sums[2:3, :], 16)
    )
    ffw_scale = lax.rsqrt(jnp.maximum(middle_sq, 0.0) / D + EPS)
    bm[s, 0:16, :] = x_in + branch * out_scale
    bm[s, 16:17, :] = gain3[...]
    bm[s, 17:18, :] = gain4[...]

    def activate(first, second):
        n = first.shape[1] // 2
        both = (first + out_scale * second) * ffw_scale
        return (jax.nn.gelu(both[:, 0:n], approximate=True) * both[:, n:2 * n]).astype(BF16)

    def gathered_sum(ref):
        return jnp.sum(ref[...].astype(F32), axis=0)

    whole(ra.at[pl.ds(0, NS - 1)], 17).wait_recv()
    first = gathered_sum(ra)
    whole(rb.at[pl.ds(0, NS - 1)], 21).wait_recv()
    main = activate(first, gathered_sum(rb))
    act[me, :, 0:FB] = main

    @pl.when(holds_extra)
    def _():
        own = extra - 4 * g
        xa[s] = wa[own]
        xb[s] = wb[own]
        whole(xa.at[pl.ds(0, NS - 1)], 18).wait_recv()
        whole(xb.at[pl.ds(0, NS - 1)], 22).wait_recv()
        act[me, :, FB:FB + 128] = activate(gathered_sum(xa), gathered_sum(xb))
        to_plane(lambda g2, s2: send(act.at[me], act.at[me], 10, {"guide": g2, "seq": s2}))

    @pl.when(jnp.logical_not(holds_extra))
    def _():
        to_plane(lambda g2, s2: send(
            act.at[me, :, pl.ds(0, FB)], act.at[me, :, pl.ds(0, FB)], 10, {"guide": g2, "seq": s2}))

    pending.append((act.at[pl.ds(0, NP - 1)], 10, holds_extra))
    pending.append((act.at[pl.ds(0, NP - 1), :, pl.ds(0, FB)], 10, jnp.logical_not(holds_extra)))

    pick_table(7, 2)
    loads[10].wait()
    blocks = 2 * (NP - 1) + EXTRA

    @pl.when(holds_extra)
    def _():
        whole(table.at[pl.ds(0, (blocks - 1) * 16), pl.ds(0, 128)], 10).wait_recv()

    @pl.when(jnp.logical_not(holds_extra))
    def _():
        whole(table.at[pl.ds(0, blocks * 16), pl.ds(0, 128)], 10).wait_recv()

    to_plane(lambda g2, s2: send(bm.at[s], bm.at[s], 9, {"seq": s2}), NS)
    pending.append((bm.at[pl.ds(0, NS - 1)], 9, None))
    owners = []
    for e in range(EXTRA):
        z2 = e // 2
        owners.append((e // 4) * NS + 4 * z2 + 2 * (e % 2) + z2 % 2)
    hidden_units = jnp.concatenate(
        [act[r, :, 0:FB] for r in range(NP)] + [act[r, :, FB:FB + 128] for r in owners], axis=1)
    b12[kv] = nt_dot(hidden_units, w_d[...])
    to_kv(lambda k2: send(b12.at[kv], b12.at[kv], 12, {"kv": k2}))
    pending.append((b12.at[pl.ds(0, NKV - 1)], 12, None))
    whole(b12.at[pl.ds(0, NKV - 1)], 12).wait_recv()
    ffw_out = (b12[0] + b12[1]) + (b12[2] + b12[3])
    b14[s] = ffw_out.astype(BF16)
    b13[me] = column_to_row(jnp.sum(ffw_out * ffw_out, axis=-1, keepdims=True))
    to_plane(lambda g2, s2: send(b14.at[s], b14.at[s], 14, {"seq": s2}), NS)
    pending.append((b14.at[pl.ds(0, NS - 1)], 14, None))
    to_plane(lambda g2, s2: send(b13.at[me], b13.at[me], 13, {"guide": g2, "seq": s2}))
    pending.append((b13.at[pl.ds(0, NP - 1)], 13, None))

    whole(bm.at[pl.ds(0, NS - 1)], 9).wait_recv()
    whole(b13.at[pl.ds(0, NP - 1)], 13).wait_recv()
    branch_scale = lax.rsqrt(row_to_column(jnp.sum(b13[...], axis=0), 16) / D + EPS)
    whole(b14.at[pl.ds(0, NS - 1)], 14).wait_recv()
    last_sq = jnp.zeros((16, WL), F32)
    for t in range(NS):
        last = bm[t, 0:16, :] + b14[t].astype(F32) * branch_scale * bm[t, 16:17, :]
        last_sq = last_sq + last * last
        rows_f[:, t * WL:(t + 1) * WL] = last * bm[t, 17:18, :]
    sq_row = column_to_row(jnp.sum(last_sq, axis=-1, keepdims=True))

    logit = nn_dot(rows_f[...].astype(BF16), table[...])
    lower = jnp.concatenate([logit[0:4, :], logit[8:12, :]], axis=0)
    upper = jnp.concatenate([logit[4:8, :], logit[12:16, :]], axis=0)
    s16[0:8, :] = jnp.where(g == 0, upper, lower)
    s16[8:9, 0:128] = sq_row
    send(s16, r16, 16, other)
    pending.append((s16, 16, None))
    keep = jnp.where(g == 0, lower, upper)
    whole(r16, 16).wait_recv()
    lanes = iota((8, 128), 1)
    rowi = iota((8, 128), 0)
    want = lax.div(rowi, 4) * 8 + 4 * g + lax.rem(rowi, 4)
    sq = jnp.sum(jnp.where(lanes == want, jnp.broadcast_to(sq_row + r16[8:9, 0:128], (8, 128)), 0.0),
                 axis=1, keepdims=True)
    final_scale = lax.rsqrt(sq / D + EPS)
    share = jnp.zeros((4, 1), F32)
    for i in range(4):
        share = jnp.where(iota((4, 1), 0) == i, guidance[4 * g + i], share)
    capped = LOGIT_CAP * jnp.tanh((keep + r16[0:8, :]) * final_scale / LOGIT_CAP)
    base_ref[...] = capped[4:8, :]
    lift_ref[...] = share * (capped[0:4, :] - capped[4:8, :])

    finish()


def on_device(
    hidden, lengths, slot_owner, allowed_ids, guidance,
    pre_attn_gain, post_attn_gain, pre_ffw_gain, post_ffw_gain, final_gain,
    query_weight, key_weight, value_weight, output_weight,
    gate_weight, up_weight, down_weight, embedding,
    cond_keys, cond_values, uncond_keys, uncond_values,
):
    lane = np.arange(HD) % (HD // 2)
    freq = jnp.asarray((THETA ** (-2.0 * lane / HD)).astype(np.float32).reshape(1, HD))
    gains = [
        gain.reshape(1, WL)
        for gain in (pre_attn_gain, post_attn_gain, pre_ffw_gain, post_ffw_gain, final_gain)
    ]
    vmem = pl.BlockSpec(memory_space=pltpu.VMEM)
    hbm = pl.BlockSpec(memory_space=pl.ANY)
    base, lift = pl.pallas_call(
        step_kernel,
        out_shape=[jax.ShapeDtypeStruct((4, PICK), F32)] * 2,
        in_specs=[hbm] * 23,
        out_specs=[vmem] * 2,
        scratch_shapes=[
            pltpu.VMEM((WL, 2048), BF16),
            pltpu.VMEM((WL, 1024), BF16),
            pltpu.VMEM((WL, FFL), BF16),
            pltpu.VMEM((WL, FFL), BF16),
            pltpu.VMEM((WL, FFL), BF16),
            pltpu.VMEM((ROWS, HALF), BF16),
            pltpu.VMEM((8, 256, 512), BF16),
            pltpu.VMEM((8, 256, 512), BF16),
            pltpu.VMEM((8, 64, 512), BF16),
            pltpu.VMEM((8, 64, 512), BF16),
            pltpu.VMEM((ROWS, PICK), BF16),
            pltpu.VMEM((HALF, PICK), BF16),
            pltpu.VMEM((16, 8, 128), F32),
            pltpu.VMEM((16, 8, 128), F32),
            pltpu.VMEM((16, 8, 128), F32),
            pltpu.VMEM((16, HALF), F32),
            pltpu.VMEM((NP, 9, 128), F32),
            pltpu.VMEM((NP, 9, 128), F32),
            pltpu.VMEM((NP, 8, 128), BF16),
            pltpu.VMEM((16, 9, 128), F32),
            pltpu.VMEM((NP, 9, 128), F32),
            pltpu.VMEM((16, 8, 128), BF16),
            pltpu.VMEM((NKV, 16, WL), F32),
            pltpu.VMEM((NP, 4, 128), F32),
            pltpu.VMEM((NS, 18, WL), F32),
            pltpu.VMEM((NP, 16, FB + 128), BF16),
            pltpu.VMEM((NKV, 16, WL), F32),
            pltpu.VMEM((NP, 1, 128), F32),
            pltpu.VMEM((NS, 16, WL), BF16),
            pltpu.VMEM((9, PICK), F32),
            pltpu.VMEM((9, PICK), F32),
            *[
                pltpu.VMEM(shape, kind)
                for _ in range(2)
                for shape, kind in (
                    ((NS, 16, 2 * FB), BF16),
                    ((NS, 16, 2 * FB), BF16),
                    ((NS, 16, 2 * FB), F32),
                    ((NS, 16, 2 * FB), BF16),
                    ((NS, 16, 2 * FB), BF16),
                    ((4, 16, FB), BF16),
                    ((4, 16, FB), BF16),
                    ((4, 16, FB), F32),
                    ((4, 16, FB), BF16),
                    ((NS, 16, FB), BF16),
                )
            ],
            pltpu.SMEM((2, 8), jnp.int32),
            pltpu.SMEM((2, 8), jnp.int32),
            pltpu.SMEM((8,), F32),
            pltpu.VMEM((2, 8, WL), BF16),
            pltpu.VMEM((8, 128), jnp.int32),
            pltpu.VMEM((1, HD), F32),
            *[pltpu.VMEM((1, WL), F32)] * 5,
            pltpu.SemaphoreType.DMA((23,)),
            pltpu.SemaphoreType.DMA((24,)),
            pltpu.SemaphoreType.DMA((24,)),
        ],
        compiler_params=pltpu.CompilerParams(
            collective_id=0, has_side_effects=True, vmem_limit_bytes=60 * 1024 * 1024
        ),
        name="decode_step",
    )(
        lengths, slot_owner, guidance, hidden, allowed_ids.reshape(8, 128), freq, *gains,
        query_weight, key_weight, value_weight, output_weight.T, gate_weight, up_weight, down_weight.T,
        embedding, cond_keys, cond_values, uncond_keys, uncond_values,
    )
    return base + lift


def solution(mesh):
    return jax.shard_map(
        on_device,
        mesh=mesh,
        in_specs=(
            P(None, None, ("guide", "seq")),
            P(),
            P(),
            P(("kv", "seq")),
            P(),
            P(("guide", "seq")),
            P(("guide", "seq")),
            P(("guide", "seq")),
            P(("guide", "seq")),
            P(("guide", "seq")),
            P(("guide", "seq"), "kv"),
            P(("guide", "seq"), "kv"),
            P(("guide", "seq"), "kv"),
            P("kv", ("guide", "seq")),
            P(("guide", "seq"), "kv"),
            P(("guide", "seq"), "kv"),
            P("kv", ("guide", "seq")),
            P(("kv", "seq"), "guide"),
            P(None, ("guide", "seq"), "kv"),
            P(None, ("guide", "seq"), "kv"),
            P(None, ("guide", "seq"), "kv"),
            P(None, ("guide", "seq"), "kv"),
        ),
        out_specs=P("guide", ("kv", "seq")),
        check_vma=False,
    )
```

```python
import functools

import jax
import jax.numpy as jnp
import numpy as np
from jax import lax
from jax.experimental import pallas as pl
from jax.experimental.pallas import tpu as pltpu
from jax.sharding import PartitionSpec as P

D = 4608
H = 32
HD = 128
EPS = 1e-06
ATTN_CAP = 50.0
LOGIT_CAP = 30.0
THETA = 10000.0
MESH = pl.DeviceIdType.MESH
F32 = jnp.float32
BF16 = jnp.bfloat16
NG, NKV, NS = 2, 4, 16
NP = NG * NS
WL = D // NP
FFL = 9216
FB = 256
EXTRA = 8
ROWS = 2048
HALF = D // 2
PICK = 1024


def iota(shape, dim):
    return lax.broadcasted_iota(jnp.int32, shape, dim)


def column_to_row(col):
    n = col.shape[0]
    spread = jnp.where(iota((n, 128), 0) == iota((n, 128), 1), jnp.broadcast_to(col, (n, 128)), 0.0)
    return jnp.sum(spread, axis=0, keepdims=True)


def row_to_column(row, n, first=0):
    lanes = iota((n, 128), 1)
    picked = jnp.where(lanes == iota((n, 128), 0) + first, jnp.broadcast_to(row, (n, 128)), 0.0)
    return jnp.sum(picked, axis=1, keepdims=True)


def nt_dot(a, b):
    return lax.dot_general(a, b, (((1,), (1,)), ((), ())), preferred_element_type=F32)


def nn_dot(a, b):
    return jnp.dot(a, b, preferred_element_type=F32)


def one_hot(mask):
    return jnp.where(mask, 1.0, 0.0).astype(BF16)


def step_kernel(
    lengths_h, owner_h, guidance_h, hidden_h, ids_h, freq_h, gain0_h, gain1_h, gain2_h, gain3_h, gain4_h,
    qw_h, kw_h, vw_h, ow_h, gw_h, uw_h, dw_h, emb_h, ck_h, cv_h, uk_h, uv_h,
    base_ref, lift_ref,
    w_qkv, w_o, w_g, w_u, w_d, emb, ck, cv, uk, uv,
    pick, table, qs, ks, vs, rows_f,
    s1, r1, b2, s3, r3, b4, b5, b6, bm, act, b12, b13, b14, s16, r16,
    pa, qa, ka, sa, ra, ta, ua, va, wa, xa, pb, qb, kb, sb, rb, tb, ub, vb, wb, xb,
    lengths, owner, guidance, hidden, ids, freq, gain0, gain1, gain2, gain3, gain4,
    load_sem, send_sem, recv_sem,
):
    g = lax.axis_index("guide")
    kv = lax.axis_index("kv")
    s = lax.axis_index("seq")
    z = lax.div(s, 4)
    x = lax.rem(s, 4)
    me = g * NS + s

    loads = [
        pltpu.make_async_copy(src, dst, load_sem.at[i])
        for i, (src, dst) in enumerate(
            [
                (qw_h, w_qkv.at[:, pl.ds(0, 1024)]),
                (kw_h, w_qkv.at[:, pl.ds(1024, 512)]),
                (vw_h, w_qkv.at[:, pl.ds(1536, 512)]),
                (ck_h, ck),
                (uk_h, uk),
                (cv_h, cv),
                (uv_h, uv),
                (ow_h, w_o),
                (gw_h, w_g),
                (uw_h, w_u),
                (dw_h, w_d),
                (emb_h, emb),
                (hidden_h, hidden),
                (gain0_h, gain0),
                (lengths_h, lengths),
                (owner_h, owner),
                (guidance_h, guidance),
                (ids_h, ids),
                (freq_h, freq),
                (gain1_h, gain1),
                (gain2_h, gain2),
                (gain3_h, gain3),
                (gain4_h, gain4),
            ]
        )
    ]

    def peer(off):
        g2 = lax.rem(g + lax.div(off, 16), 2)
        z2 = lax.rem(z + lax.div(lax.rem(off, 16), 4), 4)
        x2 = lax.rem(x + lax.rem(off, 4), 4)
        return g2, z2 * 4 + x2

    def to_plane(body, count=NP):
        def one(off, carry):
            g2, s2 = peer(off)
            body(g2, s2)
            return carry

        lax.fori_loop(1, count, one, 0)

    def to_kv(body):
        for off in range(1, NKV):
            body(lax.rem(kv + off, NKV))

    def send(src, dst, i, device):
        pltpu.make_async_remote_copy(
            src_ref=src, dst_ref=dst, send_sem=send_sem.at[i], recv_sem=recv_sem.at[i],
            device_id=device, device_id_type=MESH,
        ).start()

    def whole(ref, i):
        return pltpu.make_async_remote_copy(
            src_ref=ref, dst_ref=ref, send_sem=send_sem.at[i], recv_sem=recv_sem.at[i],
            device_id={"guide": lax.rem(g + 1, 2)}, device_id_type=MESH,
        )

    pending = []

    def finish():
        for ref, i, when in pending:
            if when is None:
                whole(ref, i).wait_send()
            else:
                pl.when(when)(functools.partial(lambda ref, i: whole(ref, i).wait_send(), ref, i))

    barrier = pltpu.get_barrier_semaphore()
    to_plane(lambda g2, s2: pl.semaphore_signal(
        barrier, inc=1, device_id={"guide": g2, "seq": s2}, device_id_type=MESH))
    to_kv(lambda k2: pl.semaphore_signal(barrier, inc=1, device_id={"kv": k2}, device_id_type=MESH))

    for load in loads[12:23] + loads[0:3]:
        load.start()
    other = {"guide": lax.rem(g + 1, 2)}
    tail = NP * FB
    holds_extra = (lax.rem(x, 2) == lax.rem(z, 2)) & (lax.div(z, 2) == g)
    extra = 2 * z + lax.div(x, 2)
    set_a = (pa, qa, ka, sa, ra, ta, ua, va, wa, xa)
    set_b = (pb, qb, kb, sb, rb, tb, ub, vb, wb, xb)

    parts = ((2, 1), (3, 0))

    def ffw_product(rows, buffers, sems):
        away, came, keep, _, _, tail_away, tail_came, tail_keep, _, _ = buffers
        high = rows.astype(BF16)
        low = (rows - high.astype(F32)).astype(BF16)
        both = jnp.concatenate([high, low], axis=0)

        def product(weight, cols):
            wide = nn_dot(both, weight[:, cols])
            return wide[0:16, :] + wide[16:32, :]

        def chip_row(whose, into, dz):
            first = 4 * lax.rem(z + dz, 4)
            cols = pl.ds(pl.multiple_of((whose * NS + first) * FB, 4 * FB), 4 * FB)
            for at, weight in ((0, w_g), (1, w_u)):
                part = product(weight, cols).astype(into.dtype)
                for c in range(4):
                    into[first + c, :, at * FB:(at + 1) * FB] = part[:, c * FB:(c + 1) * FB]
            return first

        def tail_block(whose, into):
            cols = pl.ds(pl.multiple_of(tail + whose * 512, 512), 512)
            for at, weight in ((0, w_g), (1, w_u)):
                part = product(weight, cols).astype(into.dtype)
                for c in range(4):
                    into[c, :, at * 128:(at + 1) * 128] = part[:, c * 128:(c + 1) * 128]

        for i, pair in enumerate(parts):
            for dz in pair:
                first = chip_row(1 - g, away, dz)
                send(away.at[pl.ds(first, 4)], came.at[pl.ds(first, 4)], sems[i], other)
            pending.append((away.at[pl.ds(0, 8)], sems[i], None))
        tail_block(1 - g, tail_away)
        send(tail_away, tail_came, sems[2], other)
        pending.append((tail_away, sems[2], None))
        for pair in parts:
            for dz in pair:
                chip_row(g, keep, dz)
        tail_block(g, tail_keep)

    def ffw_combine(buffers, sems, i):
        _, came, keep, out, _, _, tail_came, tail_keep, tail_out, _ = buffers
        if i == 2:
            whole(tail_came, sems[2]).wait_recv()
            tail_out[...] = (tail_keep[...] + tail_came[...].astype(F32)).astype(BF16)
            return
        whole(came.at[pl.ds(0, 8)], sems[i]).wait_recv()
        for dz in parts[i]:
            rows = pl.ds(4 * lax.rem(z + dz, 4), 4)
            out[rows] = (keep[rows] + came[rows].astype(F32)).astype(BF16)

    def ffw_send(buffers, base, i):
        _, _, _, out, into, _, _, _, tail_out, tail_into = buffers
        if i < 2:
            for dz in parts[i]:
                for dx in (2, 1, 3, 0):
                    if dz or dx:
                        s2 = 4 * lax.rem(z + dz, 4) + lax.rem(x + dx, 4)
                        send(out.at[s2], into.at[s], base, {"seq": s2})
            return

        def one(q, carry):
            z2 = 2 * g + lax.div(q, 2)
            s2 = 4 * z2 + 2 * lax.rem(q, 2) + lax.rem(z2, 2)

            @pl.when(s2 != s)
            def _():
                send(tail_out.at[q], tail_into.at[s], base + 1, {"seq": s2})

            return carry

        lax.fori_loop(0, 4, one, 0)
        into[s] = out[s]
        pending.append((out.at[pl.ds(0, NS - 1)], base, None))
        pending.append((tail_out.at[pl.ds(0, 3)], base + 1, holds_extra))
        pending.append((tail_out, base + 1, jnp.logical_not(holds_extra)))

    sems_a = (6, 8, 7)
    sems_b = (19, 15, 20)

    for load in loads[12:23]:
        load.wait()
    x_in = hidden[...].astype(F32).reshape(16, WL)
    normed = (x_in * gain0[...]).astype(BF16)
    x_sq = column_to_row(jnp.sum(x_in * x_in, axis=-1, keepdims=True))
    for i in range(3):
        loads[i].wait()
    for load in loads[3:12]:
        load.start()
    part = nn_dot(normed, w_qkv[...])
    for j in range(NS):
        for k in range(NG):
            s1[k * NS + j, 0:8, :] = part[k * 8:(k + 1) * 8, j * 128:(j + 1) * 128]
            s1[k * NS + j, 8:9, :] = x_sq
    r1[me] = s1[me]

    first_row = (kv * NS + s) * ROWS

    def pick_rows(i, carry):
        base = pl.multiple_of(i * 256, 256)
        v = iota((256, 128), 0) + (first_row + base)
        for c in range(PICK // 128):
            pick[pl.ds(base, 256), c * 128:(c + 1) * 128] = one_hot(v == ids[c:c + 1, :])
        return carry

    def pick_table(first, count):
        def one(i, carry):
            cols = pl.ds(pl.multiple_of(i * 256, 256), 256)
            table[cols, :] = lax.dot_general(
                emb[:, cols], pick[...], (((0,), (0,)), ((), ())), preferred_element_type=F32
            ).astype(BF16)
            return carry

        lax.fori_loop(first, first + count, one, 0)

    turn_row = iota((8, 128), 0)
    position = jnp.zeros((8, 128), F32)
    for i in range(8):
        position = jnp.where(turn_row == i, lengths[g, i].astype(F32), position)
    angle = position * freq[...]
    cosine = jnp.cos(angle)
    sine = jnp.sin(angle)
    sine = jnp.where(iota((8, 128), 1) < 64, -sine, sine)
    pl.semaphore_wait(barrier, NP - 1 + NKV - 1)
    to_plane(lambda g2, s2: send(
        s1.at[g2 * NS + s2], r1.at[me], 0, {"guide": g2, "seq": s2}))
    pending.append((s1.at[pl.ds(0, NP - 1)], 0, None))

    lax.fori_loop(0, ROWS // 256, pick_rows, 0)
    whole(r1.at[pl.ds(0, NP - 1)], 0).wait_recv()
    total = jnp.sum(r1[...], axis=0)
    scale = lax.rsqrt(row_to_column(total[8:9, :], 8, 8 * g) / D + EPS)
    y = total[0:8, :] * scale
    turned = y * cosine + pltpu.roll(y, 64, 1) * sine
    y = jnp.where(s < 12, turned, y)
    y = jnp.where(s < 8, y * (D // H) ** (-0.5), y)
    b2[me] = y.astype(BF16)
    to_plane(lambda g2, s2: send(b2.at[me], b2.at[me], 1, {"guide": g2, "seq": s2}))
    pending.append((b2.at[pl.ds(0, NP - 1)], 1, None))

    picks = []
    r_ = iota((64, 128), 0)
    c_ = iota((64, 128), 1)
    for k in range(NG):
        held = jnp.zeros((64, 128), jnp.int32)
        for j in range(8):
            held = jnp.where(lax.div(r_, 8) == j, owner[k, j], held)
        same = lax.rem(c_, 8) == held
        head = lax.rem(r_, 8)
        blk = lax.div(c_, 8)
        picks.append((
            one_hot(same & (blk == head)),
            one_hot(same & (blk == 8 + lax.div(head, 2))),
            one_hot(same & (blk == 12 + lax.div(head, 2))),
        ))
    block = me
    limits = []
    for k, span in ((0, 256), (1, 64)):
        limit = jnp.zeros((64, span), jnp.int32)
        row = lax.div(iota((64, span), 0), 8)
        for j in range(8):
            limit = jnp.where(row == j, lengths[k, owner[k, j]], limit)
        limits.append(iota((64, span), 1) + block * span < limit)

    loads[8].wait()
    loads[9].wait()
    ffw_product(x_in * gain2[...], set_a, sems_a)
    for i in range(3, 7):
        loads[i].wait()
    whole(b2.at[pl.ds(0, NP - 1)], 1).wait_recv()
    gathered = b2[...].astype(F32).reshape(NG, 128, 128).astype(BF16)
    lane_head = lax.div(lax.rem(iota((64, 128), 0), 8), 2)
    holds_tile = g == lax.rem(s, 2)

    def send_tiles(first):
        def one(off, carry):
            i = first + lax.rem(s + off, 8)

            @pl.when(jnp.logical_or(i != s, jnp.logical_not(holds_tile)))
            def _():
                send(s3.at[i], r3.at[me], 2, {"guide": lax.rem(i, 2), "seq": i})

            return carry

        lax.fori_loop(0, 8, one, 0)

    for k, span, keys, values in ((0, 256, ck, cv), (1, 64, uk, uv)):
        q = nn_dot(picks[k][0], gathered[k])
        for j in range(8):
            qs[k * 8 + j] = q[j * 8:(j + 1) * 8, :]
        wide = [jnp.where(lane_head == b, q, 0.0) for b in range(4)]
        scores = []
        for j in range(8):
            qj = jnp.concatenate([w[j * 8:(j + 1) * 8, :] for w in wide], axis=1).astype(BF16)
            scores.append(nt_dot(qj, keys[j]))
        score = jnp.concatenate(scores, axis=0)
        prob = jnp.where(limits[k], jnp.exp(ATTN_CAP * jnp.tanh(score / ATTN_CAP)), 0.0)
        denom = jnp.sum(prob, axis=1, keepdims=True)
        for j in range(8):
            pj = prob[j * 8:(j + 1) * 8, :].astype(BF16)
            full = nn_dot(pj, values[j])
            mine = jnp.zeros((8, 128), F32)
            for b in range(4):
                mine = jnp.where(lane_head[0:8, :] == b, full[:, b * 128:(b + 1) * 128], mine)
            s3[k * 8 + j, 0:8, :] = mine
            s3[k * 8 + j, 8:9, :] = column_to_row(denom[j * 8:(j + 1) * 8, :])
        send_tiles(k * 8)

    pending.append((s3.at[pl.ds(0, NS - 1)], 2, holds_tile))
    pending.append((s3, 2, jnp.logical_not(holds_tile)))
    pending.append((b2.at[pl.ds(0, NP - 1)], 3, holds_tile))

    for k in range(NG):
        kx = nn_dot(picks[k][1], gathered[k])
        vx = nn_dot(picks[k][2], gathered[k])
        for j in range(8):
            ks[k * 8 + j] = kx[j * 8:(j + 1) * 8, :]
            vs[k * 8 + j] = vx[j * 8:(j + 1) * 8, :]

    for i in range(3):
        ffw_combine(set_a, sems_a, i)
    loads[11].wait()
    pick_table(0, 1)

    @pl.when(holds_tile)
    def _():
        r3[me] = s3[s]
        own = jnp.exp(ATTN_CAP * jnp.tanh(jnp.sum(qs[s] * ks[s], axis=1, keepdims=True) / ATTN_CAP))
        whole(r3.at[pl.ds(0, NP - 1)], 2).wait_recv()
        sums = jnp.sum(r3[...], axis=0)
        numer = sums[0:8, :] + own.astype(BF16).astype(F32) * vs[s]
        den = row_to_column(sums[8:9, :], 8) + own
        b4[s] = (numer / den).astype(BF16)
        to_plane(lambda g2, s2: send(b4.at[s], b4.at[s], 3, {"guide": g2, "seq": s2}))

    r_ = iota((128, 128), 0)
    c_ = iota((128, 128), 1)
    held = jnp.zeros((128, 128), jnp.int32)
    for i in range(16):
        held = jnp.where(lax.div(c_, 8) == i, owner[i // 8, i % 8], held)
    back = one_hot(
        (lax.div(r_, 16) == lax.rem(c_, 8))
        & (lax.rem(lax.div(r_, 8), 2) == lax.div(c_, 64))
        & (lax.rem(r_, 8) == held)
    )
    pick_table(1, 2)
    loads[7].wait()

    @pl.when(holds_tile)
    def _():
        whole(b4.at[pl.ds(0, NS - 1)], 3).wait_recv()

    @pl.when(jnp.logical_not(holds_tile))
    def _():
        whole(b4, 3).wait_recv()

    att = nn_dot(back, b4[...].astype(F32).reshape(128, 128).astype(BF16))
    att = jnp.concatenate([att[h * 16:(h + 1) * 16, :] for h in range(8)], axis=1).astype(BF16)
    b5[kv] = nt_dot(att, w_o[...])
    to_kv(lambda k2: send(b5.at[kv], b5.at[kv], 4, {"kv": k2}))
    pending.append((b5.at[pl.ds(0, NKV - 1)], 4, None))
    for i in range(3):
        ffw_send(set_a, 17, i)
    pick_table(3, 1)
    whole(b5.at[pl.ds(0, NKV - 1)], 4).wait_recv()
    projected = (b5[0] + b5[1]) + (b5[2] + b5[3])
    branch = projected * gain1[...]
    ffw_product(branch * gain2[...], set_b, sems_b)
    ffw_combine(set_b, sems_b, 0)
    ffw_send(set_b, 21, 0)
    b6[me, 0:1, :] = column_to_row(jnp.sum(projected * projected, axis=-1, keepdims=True))
    b6[me, 1:2, :] = column_to_row(jnp.sum(x_in * branch, axis=-1, keepdims=True))
    b6[me, 2:3, :] = column_to_row(jnp.sum(branch * branch, axis=-1, keepdims=True))
    b6[me, 3:4, :] = x_sq
    to_plane(lambda g2, s2: send(b6.at[me], b6.at[me], 5, {"guide": g2, "seq": s2}))
    pending.append((b6.at[pl.ds(0, NP - 1)], 5, None))
    for i in range(1, 3):
        ffw_combine(set_b, sems_b, i)
        ffw_send(set_b, 21, i)
    pick_table(4, 3)
    whole(b6.at[pl.ds(0, NP - 1)], 5).wait_recv()
    sums = jnp.sum(b6[...], axis=0)
    out_scale = lax.rsqrt(row_to_column(sums[0:1, :], 16) / D + EPS)
    middle_sq = (
        row_to_column(sums[3:4, :], 16)
        + 2.0 * out_scale * row_to_column(sums[1:2, :], 16)
        + out_scale * out_scale * row_to_column(sums[2:3, :], 16)
    )
    ffw_scale = lax.rsqrt(jnp.maximum(middle_sq, 0.0) / D + EPS)
    bm[s, 0:16, :] = x_in + branch * out_scale
    bm[s, 16:17, :] = gain3[...]
    bm[s, 17:18, :] = gain4[...]

    def activate(first, second):
        n = first.shape[1] // 2
        both = (first + out_scale * second) * ffw_scale
        return (jax.nn.gelu(both[:, 0:n], approximate=True) * both[:, n:2 * n]).astype(BF16)

    def gathered_sum(ref):
        return jnp.sum(ref[...].astype(F32), axis=0)

    whole(ra.at[pl.ds(0, NS - 1)], 17).wait_recv()
    first = gathered_sum(ra)
    whole(rb.at[pl.ds(0, NS - 1)], 21).wait_recv()
    main = activate(first, gathered_sum(rb))
    act[me, :, 0:FB] = main

    @pl.when(holds_extra)
    def _():
        own = extra - 4 * g
        xa[s] = wa[own]
        xb[s] = wb[own]
        whole(xa.at[pl.ds(0, NS - 1)], 18).wait_recv()
        whole(xb.at[pl.ds(0, NS - 1)], 22).wait_recv()
        act[me, :, FB:FB + 128] = activate(gathered_sum(xa), gathered_sum(xb))
        to_plane(lambda g2, s2: send(act.at[me], act.at[me], 10, {"guide": g2, "seq": s2}))

    @pl.when(jnp.logical_not(holds_extra))
    def _():
        to_plane(lambda g2, s2: send(
            act.at[me, :, pl.ds(0, FB)], act.at[me, :, pl.ds(0, FB)], 10, {"guide": g2, "seq": s2}))

    pending.append((act.at[pl.ds(0, NP - 1)], 10, holds_extra))
    pending.append((act.at[pl.ds(0, NP - 1), :, pl.ds(0, FB)], 10, jnp.logical_not(holds_extra)))

    pick_table(7, 2)
    loads[10].wait()
    blocks = 2 * (NP - 1) + EXTRA

    @pl.when(holds_extra)
    def _():
        whole(table.at[pl.ds(0, (blocks - 1) * 16), pl.ds(0, 128)], 10).wait_recv()

    @pl.when(jnp.logical_not(holds_extra))
    def _():
        whole(table.at[pl.ds(0, blocks * 16), pl.ds(0, 128)], 10).wait_recv()

    to_plane(lambda g2, s2: send(bm.at[s], bm.at[s], 9, {"seq": s2}), NS)
    pending.append((bm.at[pl.ds(0, NS - 1)], 9, None))
    owners = []
    for e in range(EXTRA):
        z2 = e // 2
        owners.append((e // 4) * NS + 4 * z2 + 2 * (e % 2) + z2 % 2)
    hidden_units = jnp.concatenate(
        [act[r, :, 0:FB] for r in range(NP)] + [act[r, :, FB:FB + 128] for r in owners], axis=1)
    b12[kv] = nt_dot(hidden_units, w_d[...])
    to_kv(lambda k2: send(b12.at[kv], b12.at[kv], 12, {"kv": k2}))
    pending.append((b12.at[pl.ds(0, NKV - 1)], 12, None))
    whole(b12.at[pl.ds(0, NKV - 1)], 12).wait_recv()
    ffw_out = (b12[0] + b12[1]) + (b12[2] + b12[3])
    b14[s] = ffw_out.astype(BF16)
    b13[me] = column_to_row(jnp.sum(ffw_out * ffw_out, axis=-1, keepdims=True))
    to_plane(lambda g2, s2: send(b14.at[s], b14.at[s], 14, {"seq": s2}), NS)
    pending.append((b14.at[pl.ds(0, NS - 1)], 14, None))
    to_plane(lambda g2, s2: send(b13.at[me], b13.at[me], 13, {"guide": g2, "seq": s2}))
    pending.append((b13.at[pl.ds(0, NP - 1)], 13, None))

    whole(bm.at[pl.ds(0, NS - 1)], 9).wait_recv()
    whole(b13.at[pl.ds(0, NP - 1)], 13).wait_recv()
    branch_scale = lax.rsqrt(row_to_column(jnp.sum(b13[...], axis=0), 16) / D + EPS)
    whole(b14.at[pl.ds(0, NS - 1)], 14).wait_recv()
    last_sq = jnp.zeros((16, WL), F32)
    for t in range(NS):
        last = bm[t, 0:16, :] + b14[t].astype(F32) * branch_scale * bm[t, 16:17, :]
        last_sq = last_sq + last * last
        rows_f[:, t * WL:(t + 1) * WL] = last * bm[t, 17:18, :]
    sq_row = column_to_row(jnp.sum(last_sq, axis=-1, keepdims=True))

    logit = nn_dot(rows_f[...].astype(BF16), table[...])
    lower = jnp.concatenate([logit[0:4, :], logit[8:12, :]], axis=0)
    upper = jnp.concatenate([logit[4:8, :], logit[12:16, :]], axis=0)
    s16[0:8, :] = jnp.where(g == 0, upper, lower)
    s16[8:9, 0:128] = sq_row
    send(s16, r16, 16, other)
    pending.append((s16, 16, None))
    keep = jnp.where(g == 0, lower, upper)
    whole(r16, 16).wait_recv()
    lanes = iota((8, 128), 1)
    rowi = iota((8, 128), 0)
    want = lax.div(rowi, 4) * 8 + 4 * g + lax.rem(rowi, 4)
    sq = jnp.sum(jnp.where(lanes == want, jnp.broadcast_to(sq_row + r16[8:9, 0:128], (8, 128)), 0.0),
                 axis=1, keepdims=True)
    final_scale = lax.rsqrt(sq / D + EPS)
    share = jnp.zeros((4, 1), F32)
    for i in range(4):
        share = jnp.where(iota((4, 1), 0) == i, guidance[4 * g + i], share)
    capped = LOGIT_CAP * jnp.tanh((keep + r16[0:8, :]) * final_scale / LOGIT_CAP)
    base_ref[...] = capped[4:8, :]
    lift_ref[...] = share * (capped[0:4, :] - capped[4:8, :])

    finish()


def on_device(
    hidden, lengths, slot_owner, allowed_ids, guidance,
    pre_attn_gain, post_attn_gain, pre_ffw_gain, post_ffw_gain, final_gain,
    query_weight, key_weight, value_weight, output_weight,
    gate_weight, up_weight, down_weight, embedding,
    cond_keys, cond_values, uncond_keys, uncond_values,
):
    lane = np.arange(HD) % (HD // 2)
    freq = jnp.asarray((THETA ** (-2.0 * lane / HD)).astype(np.float32).reshape(1, HD))
    gains = [
        gain.reshape(1, WL)
        for gain in (pre_attn_gain, post_attn_gain, pre_ffw_gain, post_ffw_gain, final_gain)
    ]
    vmem = pl.BlockSpec(memory_space=pltpu.VMEM)
    hbm = pl.BlockSpec(memory_space=pl.ANY)
    base, lift = pl.pallas_call(
        step_kernel,
        out_shape=[jax.ShapeDtypeStruct((4, PICK), F32)] * 2,
        in_specs=[hbm] * 23,
        out_specs=[vmem] * 2,
        scratch_shapes=[
            pltpu.VMEM((WL, 2048), BF16),
            pltpu.VMEM((WL, 1024), BF16),
            pltpu.VMEM((WL, FFL), BF16),
            pltpu.VMEM((WL, FFL), BF16),
            pltpu.VMEM((WL, FFL), BF16),
            pltpu.VMEM((ROWS, HALF), BF16),
            pltpu.VMEM((8, 256, 512), BF16),
            pltpu.VMEM((8, 256, 512), BF16),
            pltpu.VMEM((8, 64, 512), BF16),
            pltpu.VMEM((8, 64, 512), BF16),
            pltpu.VMEM((ROWS, PICK), BF16),
            pltpu.VMEM((HALF, PICK), BF16),
            pltpu.VMEM((16, 8, 128), F32),
            pltpu.VMEM((16, 8, 128), F32),
            pltpu.VMEM((16, 8, 128), F32),
            pltpu.VMEM((16, HALF), F32),
            pltpu.VMEM((NP, 9, 128), F32),
            pltpu.VMEM((NP, 9, 128), F32),
            pltpu.VMEM((NP, 8, 128), BF16),
            pltpu.VMEM((16, 9, 128), F32),
            pltpu.VMEM((NP, 9, 128), F32),
            pltpu.VMEM((16, 8, 128), BF16),
            pltpu.VMEM((NKV, 16, WL), F32),
            pltpu.VMEM((NP, 4, 128), F32),
            pltpu.VMEM((NS, 18, WL), F32),
            pltpu.VMEM((NP, 16, FB + 128), BF16),
            pltpu.VMEM((NKV, 16, WL), F32),
            pltpu.VMEM((NP, 1, 128), F32),
            pltpu.VMEM((NS, 16, WL), BF16),
            pltpu.VMEM((9, PICK), F32),
            pltpu.VMEM((9, PICK), F32),
            *[
                pltpu.VMEM(shape, kind)
                for _ in range(2)
                for shape, kind in (
                    ((NS, 16, 2 * FB), BF16),
                    ((NS, 16, 2 * FB), BF16),
                    ((NS, 16, 2 * FB), F32),
                    ((NS, 16, 2 * FB), BF16),
                    ((NS, 16, 2 * FB), BF16),
                    ((4, 16, FB), BF16),
                    ((4, 16, FB), BF16),
                    ((4, 16, FB), F32),
                    ((4, 16, FB), BF16),
                    ((NS, 16, FB), BF16),
                )
            ],
            pltpu.SMEM((2, 8), jnp.int32),
            pltpu.SMEM((2, 8), jnp.int32),
            pltpu.SMEM((8,), F32),
            pltpu.VMEM((2, 8, WL), BF16),
            pltpu.VMEM((8, 128), jnp.int32),
            pltpu.VMEM((1, HD), F32),
            *[pltpu.VMEM((1, WL), F32)] * 5,
            pltpu.SemaphoreType.DMA((23,)),
            pltpu.SemaphoreType.DMA((24,)),
            pltpu.SemaphoreType.DMA((24,)),
        ],
        compiler_params=pltpu.CompilerParams(
            collective_id=0, has_side_effects=True, vmem_limit_bytes=60 * 1024 * 1024
        ),
        name="decode_step",
    )(
        lengths, slot_owner, guidance, hidden, allowed_ids.reshape(8, 128), freq, *gains,
        query_weight, key_weight, value_weight, output_weight.T, gate_weight, up_weight, down_weight.T,
        embedding, cond_keys, cond_values, uncond_keys, uncond_values,
    )
    return base + lift


def solution(mesh):
    return jax.shard_map(
        on_device,
        mesh=mesh,
        in_specs=(
            P(None, None, ("guide", "seq")),
            P(),
            P(),
            P(("kv", "seq")),
            P(),
            P(("guide", "seq")),
            P(("guide", "seq")),
            P(("guide", "seq")),
            P(("guide", "seq")),
            P(("guide", "seq")),
            P(("guide", "seq"), "kv"),
            P(("guide", "seq"), "kv"),
            P(("guide", "seq"), "kv"),
            P("kv", ("guide", "seq")),
            P(("guide", "seq"), "kv"),
            P(("guide", "seq"), "kv"),
            P("kv", ("guide", "seq")),
            P(("kv", "seq"), "guide"),
            P(None, ("guide", "seq"), "kv"),
            P(None, ("guide", "seq"), "kv"),
            P(None, ("guide", "seq"), "kv"),
            P(None, ("guide", "seq"), "kv"),
        ),
        out_specs=P("guide", ("kv", "seq")),
        check_vma=False,
    )
```
